128 devices in a mesh: row: 16 (over z, y), col: 8 (over x, core).
Axes of the slice: x: 4, y: 4, z: 4, core: 2. Of those that a mesh axis runs over, the one named last changes fastest.
Arguments:
- tile_values: float32 [16384, 128, 128], P(('row', 'col')), may hold values from -0.125 to 0.125
- tile_owner: int32 [16384, 1], P(('row', 'col')), may hold values from 0 to 127; in each aligned block of 128 rows (0 to 127, 128 to 255, ...) at most 2 rows name the same one
- tile_row: int32 [16384], P(('row', 'col')), may hold values from 0 to 23
- tile_col: int32 [16384], P(('row', 'col')), may hold values from 0 to 47
- tile_count: int32 [128], P(('row', 'col')), may hold values from 96 to 128, as said below
- relaxation: float32 [49152], P(('row', 'col')), may hold values from 0.3 to 1
- driving: float32 [49152, 64], P(('row', 'col')), may hold values from 0.2 to 2
- heat_weight: float32 [49152], P(('row', 'col')), may hold values from 0.1 to 3
Outputs:
- mode_flux: float32 [49152, 64], P(('row', 'col'))
- conductivity: float32 [64], replicated
The draws below stay inside these ranges and needn't reach their ends.
Inputs may be any that keep to these rules, and one draw needn't show every extreme that they name: `tile_owner`: owner d stands for row index d // 8 and column index d % 8. Among the 128 slots of one device no owner appears more than 2 times; in some device some owner appears exactly 2 times; every owner appears somewhere. Device d's slots below tile_count[d] are used, the rest are ignored; some device uses all 128.
All inputs are finite; a program needn't handle non-finite values.
Results may differ from the reference program's by a relative error of at most 0.0001.
Values sent between devices are 32-bit elements; how exact they have to be, the bound alone decides.
A program may use at most 128 MiB of HBM per device.

```python
import math
import jax
import jax.numpy as jnp
import numpy as np
from jax import lax

TILE = 128
TEMPS = 64
ITERS = 3
ROWT_DEV = 24
TILES_DEV = 128
MODES = 49152
COLT_DEV = 48
CAP = 2
N_ROW = 16
N_COL = 8
DEVICES = 128


def draw_tile_count(key, part):
    counts = jax.random.randint(jax.random.fold_in(key, 11), (N_ROW * N_COL,), max(1, 3 * TILES_DEV // 4), TILES_DEV + 1)
    chosen = jax.random.randint(jax.random.fold_in(key, 12), (), 0, N_ROW * N_COL)
    return counts.at[chosen].set(TILES_DEV).astype(jnp.int32)


def touch_ends(result, key, low, high):
    longest = result.shape.index(max(result.shape))
    spots = []
    for shift in (0, 1):
        where = [jax.random.randint(jax.random.fold_in(key, axis), (), 0, length) for axis, length in enumerate(result.shape)]
        where[longest] = (where[longest] + shift) % result.shape[longest]
        spots.append(tuple(where))
    return result.at[spots[0]].set(low).at[spots[1]].set(high)


def block_scale(own_key, extent, pieces, smallest, top_value):
    level, own = 1.0, jax.random.fold_in(own_key, 6)
    for dim, blocks in pieces:
        steps = jnp.exp(jax.random.uniform(jax.random.fold_in(own, dim), (blocks,), jnp.float32, smallest / len(pieces), top_value / len(pieces)))
        level = level * jnp.repeat(steps, extent[dim] // blocks).reshape([-1 if axis == dim else 1 for axis in range(len(extent))])
    return level


def assign_block(rng, own, number, rows, number_of, top, reach, skew):
    order = jax.random.permutation(rng, number_of)
    packed, ordinary = shares(number_of, rows * top, reach, skew, True), shares(number_of, rows * top, reach, skew, False)
    places = jnp.arange(number_of)

    def named(sizes, rotation):
        used = int((sizes > 0).sum())
        fixed = max(1, used // 4)
        shifted = fixed + (places - fixed + rotation * (used - fixed)) % max(1, number_of - fixed)
        return jnp.zeros((number_of,), jnp.int32).at[order[jnp.where(places < fixed, places, shifted)]].set(jnp.asarray(sizes, jnp.int32))

    sizes = jnp.where(number % 4 == 0, named(packed, number // 4), named(ordinary, number - number // 4 - 1))
    mixed = jax.random.permutation(jax.random.fold_in(own, 3), number_of)
    giver, sink = mixed[0:number_of // 2 * 2:2], mixed[1:number_of // 2 * 2:2]
    room = jnp.minimum(sizes[giver] - 1, reach - sizes[sink]) // 2
    room = jnp.where((giver == order[0]) | (sink == order[0]) | (sizes[sink] == 0), 0, jnp.maximum(room, 0))
    shifted = jax.random.randint(jax.random.fold_in(own, 4), (number_of // 2,), 0, 1 << 20) % (room + 1)
    sizes = sizes.at[giver].add(-shifted).at[sink].add(shifted)
    items = jnp.searchsorted(jnp.cumsum(sizes), jnp.arange(rows * top), side="right").astype(jnp.int32)
    listing = items.reshape(top, rows).T
    listing = listing[jax.random.permutation(jax.random.fold_in(own, 1), rows)]
    rotation = jax.random.randint(jax.random.fold_in(own, 2), (rows, 1), 0, top)
    return jnp.take_along_axis(listing, (jnp.arange(top)[None, :] + rotation) % top, axis=1)


def shares(amount, total, most, lean, full):
    loads = [(1 << 20) // math.isqrt(standing ** lean) + 1 for standing in range(1, amount + 1)]
    largest = most if full else min(most, max(-(-total // amount), total * loads[0] // sum(loads)))
    least = 1 if total - largest >= amount - 1 else 0
    holding, spare = [largest] + [least] * (amount - 1), total - largest - least * (amount - 1)
    while spare > 0:
        candidates = [i for i in range(1, amount) if holding[i] < largest] or [i for i in range(1, amount) if holding[i] < most]
        pool, budget = sum([loads[i] for i in candidates]), spare
        for i in candidates:
            extra = min(most - holding[i], max(1, budget * loads[i] // pool), spare)
            holding[i] = holding[i] + extra
            spare = spare - extra
    return np.array(holding)


def centred(key, extent, width, limit, split=(), held_as=jnp.bfloat16):
    array = width * jax.random.normal(key, extent, jnp.float32)
    if split:
        array = array * block_scale(key, extent, split, -0.22, 0.18)
    return jnp.clip(array, -limit, limit).astype(held_as)


def setup_inputs(seed: int = 0) -> dict:
    key_list = jax.random.split(jax.random.key(seed), 9)
    tile_values = centred(key_list[0], (DEVICES * TILES_DEV, TILE, TILE), (0.6 / (TILE * DEVICES * TILES_DEV // (ROWT_DEV * N_ROW)) ** 0.5), 0.125, ((0, 128),), jnp.float32)
    tile_owner_keys = jax.random.split(jax.random.fold_in(key_list[1], 1), (DEVICES * TILES_DEV) // TILES_DEV)
    tile_owner_turns = jax.random.permutation(jax.random.fold_in(key_list[1], 3), (DEVICES * TILES_DEV) // TILES_DEV)
    tile_owner = jax.vmap(lambda own, number: assign_block(jax.random.fold_in(key_list[1], 2), own, number, TILES_DEV, DEVICES, 1, CAP, 2))(tile_owner_keys, tile_owner_turns).reshape((DEVICES * TILES_DEV, 1))
    tile_row = touch_ends(jax.random.randint(key_list[2], (DEVICES * TILES_DEV,), 0, ROWT_DEV), jax.random.fold_in(key_list[2], 1), 0, ROWT_DEV - 1).astype(jnp.int32)
    tile_col = touch_ends(jax.random.randint(key_list[3], (DEVICES * TILES_DEV,), 0, COLT_DEV), jax.random.fold_in(key_list[3], 1), 0, COLT_DEV - 1).astype(jnp.int32)
    tile_count = draw_tile_count(jax.random.fold_in(key_list[8], 71), 0)
    relaxation = jnp.clip(jnp.exp(math.log(1.0) - 1.2039728 * jax.random.uniform(key_list[5], (MODES,), jnp.float32) ** block_scale(key_list[5], (MODES,), ((0, 128),), -0.2, 0.2)), 0.3, 1.0)
    driving = jnp.clip(0.2 + 1.8 * jax.random.uniform(key_list[6], (MODES, TEMPS), jnp.float32) ** block_scale(key_list[6], (MODES, TEMPS), ((0, 128),), -0.2, 0.2), 0.2, 2.0)
    heat_weight = jnp.clip(jnp.exp(math.log(3.0) - 3.4011974 * jax.random.uniform(key_list[7], (MODES,), jnp.float32) ** block_scale(key_list[7], (MODES,), ((0, 128),), -0.2, 0.2)), 0.1, 3.0)
    return dict(tile_values=tile_values, tile_owner=tile_owner, tile_row=tile_row, tile_col=tile_col, tile_count=tile_count, relaxation=relaxation, driving=driving, heat_weight=heat_weight)


def reference(tile_values, tile_owner, tile_row, tile_col, tile_count, relaxation, driving, heat_weight):
    devices = N_ROW * N_COL
    per_device = TILES_DEV
    per_group = ROWT_DEV // N_COL
    owners = tile_owner[:, 0]
    slots = jnp.arange(devices * per_device, dtype=jnp.int32)
    is_used = (slots % per_device) < tile_count[slots // per_device]
    grow = (owners // N_COL) * ROWT_DEV + tile_row
    gcol = ((tile_col // per_group) * N_COL + owners % N_COL) * per_group + tile_col % per_group
    weights = jnp.where(is_used[:, None, None], tile_values, jnp.zeros_like(tile_values)).astype(jnp.float32)
    num_tiles = MODES // TILE

    def apply_matrix(flux_now):
        tiled = flux_now.reshape(num_tiles, TILE, TEMPS)

        def step_one(accum, item):
            weight_block, rows_idx, cols_idx = item
            product = jnp.einsum("sij,sjk->sik", weight_block, tiled[cols_idx], precision=lax.Precision.HIGHEST)
            return accum.at[rows_idx].add(product), None

        start_acc = jnp.zeros((num_tiles, TILE, TEMPS), jnp.float32)
        accum, _ = lax.scan(step_one, start_acc, (weights.reshape(devices, per_device, TILE, TILE), grow.reshape(devices, per_device), gcol.reshape(devices, per_device)))
        return accum.reshape(MODES, TEMPS)

    mode_flux = relaxation[:, None] * driving
    for sweep in range(ITERS):
        mode_flux = relaxation[:, None] * (driving + apply_matrix(mode_flux))
    conductivity = jnp.sum(heat_weight[:, None] * mode_flux, axis=0) / jnp.sum(heat_weight)
    return mode_flux, conductivity
```

```python
import jax
import jax.numpy as jnp
from jax import lax
from jax.experimental import pallas as pl
from jax.experimental.pallas import tpu as pltpu
from jax.sharding import Mesh
from jax.sharding import PartitionSpec as P

ITERS = 3
TILE = 128
TEMPS = 64
ROWT_DEV = 24
SLOTS = 128
RING = 4
CHIPS = 64
COLORS = 3
HALF = COLORS * CHIPS
AXES = ("z", "y", "x", "core")
ORDERS = (("x", "y", "z"), ("y", "z", "x"), ("z", "x", "y"))
RECV_BASE = {2: 0, 1: 48, 0: 60}
RECV_TILES = 63
MESH = pl.DeviceIdType.MESH


def place(coords, color):
    order = ORDERS[color]
    return coords[order[0]] + 4 * coords[order[1]] + 16 * coords[order[2]]


def half_of(ref, first, tiles, h):
    if tiles == 1:
        return ref.at[pl.ds(first, 1), pl.ds((TEMPS // 2) * h, TEMPS // 2)]
    return ref.at[pl.ds(first + h * (tiles // 2), tiles // 2)]


def add_half(dst, first, src, src_first, tiles, h):
    if tiles == 1:
        rows = pl.ds((TEMPS // 2) * h, TEMPS // 2)
        dst[first, rows] = dst[first, rows] + src[src_first, rows]
        return

    @pl.loop(0, tiles // 2)
    def _(t):
        k = t + h * (tiles // 2)
        dst[first + k] = dst[first + k] + src[src_first + k]


def kernel(
    order_ref,
    xs_ref,
    first_ref,
    last_ref,
    tiles_hbm,
    driving_ref,
    relax_ref,
    heat_ref,
    flux_ref,
    cond_ref,
    stage,
    t_hi,
    t_lo,
    x_all,
    sums,
    y_own,
    y_pair,
    r_pair,
    r_ring,
    c_recv,
    stage_sem,
    ag_send,
    ag_recv,
    fw_send,
    fw_recv,
    pr_send,
    pr_recv,
    rs_send,
    rs_recv,
    c_send,
    c_recv_sem,
):
    coords = {a: lax.axis_index(a) for a in AXES}
    core = coords["core"]
    mate = {"core": 1 - core}

    def at(axis, step):
        return {axis: lax.rem(coords[axis] + step, RING)}

    barrier = pltpu.get_barrier_semaphore()
    for axis in ("x", "y", "z"):
        for step in (1, 2, 3):
            pl.semaphore_signal(barrier, inc=1, device_id=at(axis, step), device_id_type=MESH)
    pl.semaphore_signal(barrier, inc=1, device_id=mate, device_id_type=MESH)
    pl.semaphore_wait(barrier, 10)

    def remote(src, dst, ssem, rsem, device):
        return pltpu.make_async_remote_copy(
            src_ref=src, dst_ref=dst, send_sem=ssem, recv_sem=rsem, device_id=device, device_id_type=MESH
        )

    load = pltpu.make_async_copy(tiles_hbm, stage, stage_sem)
    load.start()

    own = [(c * 2 + core) * CHIPS + place(coords, c) for c in range(COLORS)]
    for c in range(COLORS):
        x_all[own[c]] = relax_ref[c] * driving_ref[c]
    sums[SLOTS] = jnp.zeros((TEMPS, TILE), jnp.float32)

    def block(c, p, step):
        order = ORDERS[c]
        base = lax.rem(coords[order[p]] + step, RING) * 4**p
        for q in range(p + 1, 3):
            base = base + coords[order[q]] * 4**q
        return base

    def split_tiles():
        load.wait()

        @pl.loop(0, SLOTS)
        def _(j):
            tile = stage[order_ref[j]]
            hi = tile.astype(jnp.bfloat16)
            t_hi[j] = hi
            t_lo[j] = (tile - hi.astype(jnp.float32)).astype(jnp.bfloat16)

    def gather(sweep):
        sends = []

        def xblock(c, p, step):
            return (c * 2 + core) * CHIPS + block(c, p, step)

        def forward(c, piece, step):
            ref = x_all.at[pl.ds(xblock(c, 2, step), 16)]
            copy = remote(ref, ref, fw_send.at[c, piece], fw_recv.at[c, piece], mate)
            copy.start()
            return copy

        forwards = []
        for p in range(3):
            n = 4**p
            copies = {}

            def send(c, way, part, step, h, n=n, p=p, copies=copies):
                ref = half_of(x_all, xblock(c, p, step), n, h)
                copy = remote(
                    ref, ref, ag_send.at[c, p, way, part], ag_recv.at[c, p, way, part], at(ORDERS[c][p], 1 + 2 * way)
                )
                copy.start()
                copies[c, way, part] = copy
                sends.append(copy)

            for c in range(COLORS):
                for part in range(2):
                    send(c, 0, part, 0, part)
                    send(c, 1, part, 0, 1 - part)
            if p == 2:
                for c in range(COLORS):
                    forwards.append(forward(c, 0, 0))
                pl.when(sweep == 0)(split_tiles)
            for c in range(COLORS):
                copies[c, 0, 0].wait_recv()
                send(c, 0, 2, 3, 0)
                copies[c, 1, 0].wait_recv()
                send(c, 1, 2, 1, 1)
            for c in range(COLORS):
                copies[c, 0, 1].wait_recv()
                copies[c, 1, 1].wait_recv()
                if p == 2:
                    forwards.append(forward(c, 1, 3))
                    forwards.append(forward(c, 2, 1))
            for c in range(COLORS):
                copies[c, 0, 2].wait_recv()
                copies[c, 1, 2].wait_recv()
                if p == 2:
                    forwards.append(forward(c, 3, 2))
        for copy in forwards:
            copy.wait_recv()
        for copy in forwards + sends:
            copy.wait_send()

    nt = (((1,), (1,)), ((), ()))

    def multiply():
        unroll = 8

        def some(g, acc):
            for u in range(unroll):
                j = g * unroll + u
                x = x_all[xs_ref[j]]
                hi = x.astype(jnp.bfloat16)
                lo = (x - hi.astype(jnp.float32)).astype(jnp.bfloat16)
                th = t_hi[j]
                prod = (
                    lax.dot_general(hi, th, nt, preferred_element_type=jnp.float32)
                    + lax.dot_general(lo, th, nt, preferred_element_type=jnp.float32)
                    + lax.dot_general(hi, t_lo[j], nt, preferred_element_type=jnp.float32)
                )
                acc = jnp.where(first_ref[j] != 0, 0.0, acc) + prod
                sums[j] = acc
            return acc

        lax.fori_loop(0, SLOTS // unroll, some, jnp.zeros((TEMPS, TILE), jnp.float32))

    def scatter():
        pair = []
        for c in range(COLORS):

            @pl.loop(0, CHIPS)
            def _(t, c=c):
                y_pair[c * CHIPS + t] = sums[last_ref[(c * 2 + 1 - core) * CHIPS + t]]

            copy = remote(
                y_pair.at[pl.ds(c * CHIPS, CHIPS)],
                r_pair.at[pl.ds(c * CHIPS, CHIPS)],
                pr_send.at[c],
                pr_recv.at[c],
                mate,
            )
            copy.start()
            pair.append(copy)
        for c in range(COLORS):

            @pl.loop(0, CHIPS)
            def _(t, c=c):
                y_own[c * CHIPS + t] = sums[last_ref[(c * 2 + core) * CHIPS + t]]

        sends = list(pair)
        for p in (2, 1, 0):
            n = 4**p
            copies = {}

            def yblock(c, step, p=p):
                return c * CHIPS + block(c, p, step)

            def recv(c, which, p=p, n=n):
                return c * RECV_TILES + RECV_BASE[p] + which * n

            def send(c, way, part, src, dst, p=p, copies=copies):
                copy = remote(
                    src, dst, rs_send.at[c, p, way, part], rs_recv.at[c, p, way, part], at(ORDERS[c][p], 1 + 2 * way)
                )
                copy.start()
                copies[c, way, part] = copy
                sends.append(copy)

            for c in range(COLORS):
                if p == 2:
                    pair[c].wait_recv()

                    @pl.loop(0, CHIPS)
                    def _(t, c=c):
                        y_own[c * CHIPS + t] = y_own[c * CHIPS + t] + r_pair[c * CHIPS + t]

                for way, near in ((0, 1), (1, 3)):
                    send(c, way, 0, half_of(y_own, yblock(c, 2), n, way), half_of(r_ring, recv(c, 2), n, way))
                    send(c, way, 1, half_of(y_own, yblock(c, near), n, 1 - way), half_of(r_ring, recv(c, way), n, 1 - way))
            for c in range(COLORS):
                for way, near in ((0, 1), (1, 3)):
                    copies[c, way, 0].wait_recv()
                    add_half(y_own, yblock(c, near), r_ring, recv(c, 2), n, way)
                    send(c, way, 2, half_of(y_own, yblock(c, near), n, way), half_of(r_ring, recv(c, way), n, way))
            for c in range(COLORS):
                for part in (1, 2):
                    for way in (0, 1):
                        copies[c, way, part].wait_recv()

                @pl.loop(0, n)
                def _(t, c=c):
                    k = yblock(c, 0) + t
                    y_own[k] = y_own[k] + (r_ring[recv(c, 0) + t] + r_ring[recv(c, 1) + t])

        for copy in sends:
            copy.wait_send()

    def sweep_once(sweep, carry):
        gather(sweep)
        multiply()
        scatter()
        for c in range(COLORS):
            flux = relax_ref[c] * (driving_ref[c] + y_own[c * CHIPS + place(coords, c)])
            flux_ref[c] = flux
            x_all[own[c]] = flux
        return carry

    lax.fori_loop(0, ITERS, sweep_once, 0)

    part = heat_ref[0] * flux_ref[0] + heat_ref[1] * flux_ref[1] + heat_ref[2] * flux_ref[2]
    weight = heat_ref[0] + heat_ref[1] + heat_ref[2]
    total = jnp.concatenate([part, jnp.broadcast_to(weight, (8, TILE))], axis=0)
    copies = []
    for s, axis in enumerate(("core", "x", "y", "z")):
        size = 2 if axis == "core" else RING
        here = coords[axis]
        c_recv[s * RING + here] = total
        stage_copies = []
        for step in range(1, size):
            peer = {axis: lax.rem(here + step, size)}
            ref = c_recv.at[s * RING + here]
            copy = remote(ref, ref, c_send.at[s, step - 1], c_recv_sem.at[s, step - 1], peer)
            copy.start()
            stage_copies.append(copy)
        for copy in stage_copies:
            copy.wait_recv()
        copies += stage_copies
        total = c_recv[s * RING] + c_recv[s * RING + 1]
        if size == RING:
            total = total + (c_recv[s * RING + 2] + c_recv[s * RING + 3])
    for copy in copies:
        copy.wait_send()
    sums_out = jnp.sum(total, axis=1, keepdims=True)
    cond_ref[...] = jnp.broadcast_to(sums_out[:TEMPS] / sums_out[TEMPS : TEMPS + 1], (TEMPS, TILE))


def index_of(device, color):
    coords = {"z": device // 32, "y": device // 8 % 4, "x": device // 2 % 4}
    spot = jnp.where(color == 0, place(coords, 0), jnp.where(color == 1, place(coords, 1), place(coords, 2)))
    return (color * 2 + device % 2) * CHIPS + spot


def shards(tile_values, tile_owner, tile_row, tile_col, tile_count, relaxation, driving, heat_weight):
    owner = tile_owner[:, 0]
    slots = jnp.arange(SLOTS, dtype=jnp.int32)
    is_used = slots < tile_count[0]
    row = (owner // 8) * ROWT_DEV + tile_row
    key = jnp.where(is_used, index_of(row // COLORS, row % COLORS), 2 * HALF)
    xs = index_of((tile_col // COLORS) * 8 + owner % 8, tile_col % COLORS)
    before = (key[None, :] < key[:, None]) | ((key[None, :] == key[:, None]) & (slots[None, :] < slots[:, None]))
    rank = jnp.sum(before.astype(jnp.int32), axis=1)
    is_here = (rank[None, :] == slots[:, None]).astype(jnp.int32)
    order = jnp.sum(is_here * slots[None, :], axis=1)
    xs = jnp.sum(is_here * xs[None, :], axis=1)
    keys = jnp.sum(is_here * key[None, :], axis=1)
    first = (keys != jnp.concatenate([jnp.full((1,), -1, jnp.int32), keys[:-1]])).astype(jnp.int32)
    rows = jnp.arange(2 * HALF, dtype=jnp.int32)
    upto = jnp.sum((key[None, :] <= rows[:, None]).astype(jnp.int32), axis=1)
    has = jnp.any(key[None, :] == rows[:, None], axis=1)
    last = jnp.where(has, upto - 1, SLOTS)

    smem = pl.BlockSpec(memory_space=pltpu.SMEM)
    vmem = pl.BlockSpec(memory_space=pltpu.VMEM)
    f32 = jnp.float32
    dma = pltpu.SemaphoreType.DMA
    flux, cond = pl.pallas_call(
        kernel,
        out_shape=(
            jax.ShapeDtypeStruct((COLORS, TEMPS, TILE), f32),
            jax.ShapeDtypeStruct((TEMPS, TILE), f32),
        ),
        in_specs=[smem] * 4 + [pl.BlockSpec(memory_space=pl.ANY)] + [vmem] * 3,
        out_specs=(vmem, vmem),
        scratch_shapes=[
            pltpu.VMEM((SLOTS, TILE, TILE), f32),
            pltpu.VMEM((SLOTS, TILE, TILE), jnp.bfloat16),
            pltpu.VMEM((SLOTS, TILE, TILE), jnp.bfloat16),
            pltpu.VMEM((2 * HALF, TEMPS, TILE), f32),
            pltpu.VMEM((SLOTS + 1, TEMPS, TILE), f32),
            pltpu.VMEM((HALF, TEMPS, TILE), f32),
            pltpu.VMEM((HALF, TEMPS, TILE), f32),
            pltpu.VMEM((HALF, TEMPS, TILE), f32),
            pltpu.VMEM((COLORS * RECV_TILES, TEMPS, TILE), f32),
            pltpu.VMEM((4 * RING, TEMPS + 8, TILE), f32),
            dma,
            dma((COLORS, 3, 2, 3)),
            dma((COLORS, 3, 2, 3)),
            dma((COLORS, 4)),
            dma((COLORS, 4)),
            dma((COLORS,)),
            dma((COLORS,)),
            dma((COLORS, 3, 2, 3)),
            dma((COLORS, 3, 2, 3)),
            dma((4, 3)),
            dma((4, 3)),
        ],
        compiler_params=pltpu.CompilerParams(
            collective_id=0, has_side_effects=True, vmem_limit_bytes=67043328
        ),
        name="solve",
    )(
        order,
        xs,
        first,
        last,
        tile_values,
        driving.reshape(COLORS, TILE, TEMPS).transpose(0, 2, 1),
        relaxation.reshape(COLORS, 1, TILE),
        heat_weight.reshape(COLORS, 1, TILE),
    )
    mode_flux = flux.transpose(0, 2, 1).reshape(COLORS * TILE, TEMPS)
    return mode_flux, cond[:, 0]


def solution(mesh):
    torus = Mesh(mesh.devices.reshape(4, 4, 4, 2), AXES)
    placed = (
        P(AXES, None, None),
        P(AXES, None),
        P(AXES),
        P(AXES),
        P(AXES),
        P(AXES),
        P(AXES, None),
        P(AXES),
    )
    return jax.shard_map(
        shards, mesh=torus, in_specs=placed, out_specs=(P(AXES, None), P()), check_vma=False
    )
```

```python
import jax
import jax.numpy as jnp
from jax import lax
from jax.experimental import pallas as pl
from jax.experimental.pallas import tpu as pltpu
from jax.sharding import Mesh
from jax.sharding import PartitionSpec as P

ITERS = 3
TILE = 128
TEMPS = 64
ROWT_DEV = 24
SLOTS = 128
RING = 4
CHIPS = 64
COLORS = 3
HALF = COLORS * CHIPS
AXES = ("z", "y", "x", "core")
ORDERS = (("x", "y", "z"), ("y", "z", "x"), ("z", "x", "y"))
GROUPS = (2, 1, 3, 0)
RING_TILES = 63
NT = (((1,), (1,)), ((), ()))
MESH = pl.DeviceIdType.MESH


def place(coords, color, strides):
    order = ORDERS[color]
    return coords[order[0]] + strides[0] * coords[order[1]] + strides[1] * coords[order[2]]


X_STRIDES = (4, 16)
Y_STRIDES = (16, 4)


def kernel(
    order_ref,
    xs_ref,
    first_ref,
    last_ref,
    tiles_hbm,
    driving_ref,
    relax_ref,
    heat_ref,
    flux_ref,
    cond_ref,
    stage,
    t_hi,
    t_lo,
    x_all,
    sums,
    y_own,
    y_pair,
    r_pair,
    r_ring,
    c_all,
    stage_sem,
    g1_send,
    g1_recv,
    g2_send,
    g2_recv,
    g3_send,
    g3_recv,
    fw_send,
    fw_recv,
    pr_send,
    pr_recv,
    s3_send,
    s3_recv,
    s2_send,
    s2_recv,
    s1_send,
    s1_recv,
    c_send,
    c_recv,
):
    coords = {a: lax.axis_index(a) for a in AXES}
    core = coords["core"]
    mate = {"core": 1 - core}

    def at(axis, step):
        return {axis: lax.rem(coords[axis] + step, RING)}

    def chip_row(k):
        spot = lax.rem(coords["x"] * 2 + core + k, 8)
        return {"x": spot // 2, "core": lax.rem(spot, 2)}

    peers = [at(axis, step) for axis in ("y", "z") for step in (1, 2, 3)]
    peers += [chip_row(k) for k in range(1, 8)]
    barrier = pltpu.get_barrier_semaphore()
    for peer in peers:
        pl.semaphore_signal(barrier, inc=1, device_id=peer, device_id_type=MESH)
    load = pltpu.make_async_copy(tiles_hbm, stage, stage_sem)
    load.start()

    def lanes(c):
        return slice(c * TILE, (c + 1) * TILE)

    own = [(c * 2 + core) * CHIPS + place(coords, c, X_STRIDES) for c in range(COLORS)]
    for c in range(COLORS):
        x_all[own[c]] = relax_ref[:, lanes(c)] * driving_ref[:, lanes(c)]
    sums[SLOTS] = jnp.zeros((TEMPS, TILE), jnp.float32)
    pl.semaphore_wait(barrier, len(peers))

    def along(c, p, step):
        return lax.rem(coords[ORDERS[c][p]] + step, RING)

    sends = []

    def remote(src, dst, ssem, rsem, device):
        copy = pltpu.make_async_remote_copy(
            src_ref=src, dst_ref=dst, send_sem=ssem, recv_sem=rsem, device_id=device, device_id_type=MESH
        )
        copy.start()
        sends.append(copy)
        return copy

    def drain():
        for copy in sends:
            copy.wait_send()
        sends.clear()

    def to(c, p, way):
        return at(ORDERS[c][p], 1 + 2 * way)

    def split_tiles():
        load.wait()

        @pl.loop(0, SLOTS)
        def _(j):
            tile = stage[order_ref[j]]
            hi = tile.astype(jnp.bfloat16)
            t_hi[j] = hi
            t_lo[j] = (tile - hi.astype(jnp.float32)).astype(jnp.bfloat16)

    everyone = range(COLORS)
    ways = (0, 1)

    def gather(sweep):
        near, far, wide, forwards = {}, {}, {}, []
        wide2 = {}

        def xt(c, j, g):
            return (c * 2 + core) * CHIPS + along(c, 2, j) * 16 + along(c, 1, g) * 4

        def tiles(first, count):
            return x_all.at[pl.ds(first, count)]

        def forward(c, piece, first, count):
            ref = tiles(first, count)
            forwards.append(remote(ref, ref, fw_send.at[c, piece], fw_recv.at[c, piece], mate))

        def block(c, g):
            for w in ways:
                ref = tiles(xt(c, 0, g), 4)
                wide[c, g, w] = remote(ref, ref, g3_send.at[c, g, w, 0], g3_recv.at[c, g, w, 0], to(c, 2, w))

        def relay(c, g):
            for w in ways:
                wide[c, g, w].wait_recv()
                ref = tiles(xt(c, 3 - 2 * w, g) + 2 * w, 2)
                wide2[c, g, w] = remote(ref, ref, g3_send.at[c, g, w, 1], g3_recv.at[c, g, w, 1], to(c, 2, w))
            for w in ways:
                forward(c, 1 + g * 3 + w, xt(c, 3 - 2 * w, g), 4)

        def arrived(c, g):
            for w in ways:
                wide2[c, g, w].wait_recv()
            forward(c, 3 + g * 3, xt(c, 2, g), 4)

        for c in everyone:
            for step in (1, 3, 2):
                ref = tiles(own[c], 1)
                near[c, step] = remote(
                    ref, ref, g1_send.at[c, step - 1], g1_recv.at[c, step - 1], at(ORDERS[c][0], step)
                )
        for c in everyone:
            for step in (1, 3, 2):
                near[c, step].wait_recv()
            for w in ways:
                ref = tiles(xt(c, 0, 0), 4)
                far[c, w] = remote(ref, ref, g2_send.at[c, w, 0], g2_recv.at[c, w, 0], to(c, 1, w))
        for c in everyone:
            block(c, 0)
        for c in everyone:
            for w in ways:
                far[c, w].wait_recv()
                ref = tiles(xt(c, 0, 3 - 2 * w) + 2 * w, 2)
                far[c, w] = remote(ref, ref, g2_send.at[c, w, 1], g2_recv.at[c, w, 1], to(c, 1, w))
        for g in (3, 1):
            for c in everyone:
                block(c, g)
        pl.when(sweep == 0)(split_tiles)
        for c in everyone:
            relay(c, 0)
        for c in everyone:
            for w in ways:
                far[c, w].wait_recv()
            block(c, 2)
            forward(c, 0, (c * 2 + core) * CHIPS + along(c, 2, 0) * 16, 16)
        for g in (3, 1):
            for c in everyone:
                relay(c, g)
        for c in everyone:
            arrived(c, 0)
        for c in everyone:
            relay(c, 2)
        for g in (3, 1, 2):
            for c in everyone:
                arrived(c, g)
        for copy in forwards:
            copy.wait_recv()
        drain()

    def multiply():
        unroll = 8

        def some(g, acc):
            for u in range(unroll):
                j = g * unroll + u
                x = x_all[xs_ref[j]]
                hi = x.astype(jnp.bfloat16)
                lo = (x - hi.astype(jnp.float32)).astype(jnp.bfloat16)
                both = lax.dot_general(
                    jnp.concatenate([hi, lo], axis=0), t_hi[j], NT, preferred_element_type=jnp.float32
                )
                rest = lax.dot_general(hi, t_lo[j], NT, preferred_element_type=jnp.float32)
                prod = both[:TEMPS] + both[TEMPS:] + rest
                acc = jnp.where(first_ref[j] != 0, 0.0, acc) + prod
                sums[j] = acc
            return acc

        lax.fori_loop(0, SLOTS // unroll, some, jnp.zeros((TEMPS, TILE), jnp.float32))

    def scatter():
        pair, half, full = {}, {}, {}

        def yt(c, g, j):
            return c * CHIPS + along(c, 1, g) * 16 + along(c, 2, j) * 4

        def rt(c, g):
            return c * RING_TILES + g * 12

        def give(c, g):
            first = along(c, 1, g) * 16

            @pl.loop(0, 4)
            def _(q):
                for u in range(4):
                    k = first + q * 4 + u
                    y_pair[c * CHIPS + k] = sums[last_ref[(c * 2 + 1 - core) * CHIPS + k]]

            span = pl.ds(c * CHIPS + first, 16)
            pair[c, g] = remote(y_pair.at[span], r_pair.at[span], pr_send.at[c, g], pr_recv.at[c, g], mate)

        def take(c, g):
            first = along(c, 1, g) * 16
            pair[c, g].wait_recv()

            @pl.loop(0, 4)
            def _(q):
                for u in range(4):
                    k = first + q * 4 + u
                    y_own[c * CHIPS + k] = sums[last_ref[(c * 2 + core) * CHIPS + k]] + r_pair[c * CHIPS + k]

            for w in ways:
                half[c, g, w] = remote(
                    y_own.at[pl.ds(yt(c, g, 2) + 2 * w, 2)],
                    r_ring.at[pl.ds(rt(c, g) + 2 * w, 2)],
                    s3_send.at[c, g, w, 0],
                    s3_recv.at[c, g, w, 0],
                    to(c, 2, w),
                )

        def pass_on(c, g):
            for w in ways:
                half[c, g, w].wait_recv()
                near = yt(c, g, 1 + 2 * w)
                for u in range(2 * w, 2 * w + 2):
                    y_own[near + u] = y_own[near + u] + r_ring[rt(c, g) + u]
                full[c, g, w] = remote(
                    y_own.at[pl.ds(near, 4)],
                    r_ring.at[pl.ds(rt(c, g) + 4 + 4 * w, 4)],
                    s3_send.at[c, g, w, 1],
                    s3_recv.at[c, g, w, 1],
                    to(c, 2, w),
                )

        def settle(c, g):
            for w in ways:
                full[c, g, w].wait_recv()
            here = yt(c, g, 0)
            for u in range(4):
                y_own[here + u] = y_own[here + u] + (r_ring[rt(c, g) + 4 + u] + r_ring[rt(c, g) + 8 + u])

        def take2(c):
            for w in ways:
                half[c, w] = remote(
                    y_own.at[pl.ds(yt(c, 2, 0) + 2 * w, 2)],
                    r_ring.at[pl.ds(rt(c, 4) + 2 * w, 2)],
                    s2_send.at[c, w, 0],
                    s2_recv.at[c, w, 0],
                    to(c, 1, w),
                )

        def pass_on2(c):
            for w in ways:
                half[c, w].wait_recv()
                near = yt(c, 1 + 2 * w, 0)
                for u in range(2 * w, 2 * w + 2):
                    y_own[near + u] = y_own[near + u] + r_ring[rt(c, 4) + u]
                full[c, w] = remote(
                    y_own.at[pl.ds(near, 4)],
                    r_ring.at[pl.ds(rt(c, 4) + 4 + 4 * w, 4)],
                    s2_send.at[c, w, 1],
                    s2_recv.at[c, w, 1],
                    to(c, 1, w),
                )

        def settle2(c):
            for w in ways:
                full[c, w].wait_recv()
            here = yt(c, 0, 0)
            for u in range(4):
                y_own[here + u] = y_own[here + u] + (r_ring[rt(c, 4) + 4 + u] + r_ring[rt(c, 4) + 8 + u])

        for g in GROUPS:
            for c in everyone:
                give(c, g)
        plan = (
            (take, 2),
            (take, 1),
            (pass_on, 2),
            (take, 3),
            (pass_on, 1),
            (take, 0),
            (settle, 2),
            (take2,),
            (pass_on, 3),
            (pass_on, 0),
            (settle, 1),
            (settle, 3),
            (pass_on2,),
            (settle, 0),
            (settle2,),
        )
        for act, *group in plan:
            for c in everyone:
                act(c, *group)
        last = {}
        for c in everyone:
            for step in (1, 3, 2):
                last[c, step] = remote(
                    y_own.at[pl.ds(yt(c, 0, 0) + along(c, 0, step), 1)],
                    r_ring.at[pl.ds(rt(c, 5) + step - 1, 1)],
                    s1_send.at[c, step - 1],
                    s1_recv.at[c, step - 1],
                    at(ORDERS[c][0], step),
                )
        for c in everyone:
            for step in (1, 3, 2):
                last[c, step].wait_recv()
            got = (r_ring[rt(c, 5)] + r_ring[rt(c, 5) + 1]) + r_ring[rt(c, 5) + 2]
            total = y_own[yt(c, 0, 0) + along(c, 0, 0)] + got
            flux = relax_ref[:, lanes(c)] * (driving_ref[:, lanes(c)] + total)
            flux_ref[:, lanes(c)] = flux
            x_all[own[c]] = flux
        drain()

    def sweep_once(sweep, carry):
        gather(sweep)
        multiply()
        scatter()
        return carry

    lax.fori_loop(0, ITERS, sweep_once, 0)

    part, weight = 0.0, 0.0
    for c in everyone:
        part = part + heat_ref[:, lanes(c)] * flux_ref[:, lanes(c)]
        weight = weight + heat_ref[:, lanes(c)]
    stacked = jnp.concatenate([part, jnp.broadcast_to(weight, (TILE - TEMPS, TILE))], axis=0)
    total = lax.dot_general(
        jnp.ones((8, TILE), jnp.float32),
        stacked,
        NT,
        precision=lax.Precision.HIGHEST,
        preferred_element_type=jnp.float32,
    )
    base = 0
    row = [chip_row(k) for k in range(8)]
    for s, (size, here, others) in enumerate(
        (
            (8, coords["x"] * 2 + core, row[1:]),
            (RING, coords["y"], [at("y", k) for k in (1, 2, 3)]),
            (RING, coords["z"], [at("z", k) for k in (1, 2, 3)]),
        )
    ):
        ref = c_all.at[base + here]
        ref[...] = total
        copies = [
            remote(ref, ref, c_send.at[s, k], c_recv.at[s, k], peer) for k, peer in enumerate(others)
        ]
        for copy in copies:
            copy.wait_recv()
        total = c_all[base]
        for k in range(1, size):
            total = total + c_all[base + k]
        base += size
    cond_ref[...] = total
    drain()


def index_of(device, color, strides):
    coords = {"z": device // 32, "y": device // 8 % 4, "x": device // 2 % 4}
    spots = [place(coords, c, strides) for c in range(COLORS)]
    spot = jnp.where(color == 0, spots[0], jnp.where(color == 1, spots[1], spots[2]))
    return (color * 2 + device % 2) * CHIPS + spot


def shards(tile_values, tile_owner, tile_row, tile_col, tile_count, relaxation, driving, heat_weight):
    owner = tile_owner[:, 0]
    slots = jnp.arange(SLOTS, dtype=jnp.int32)
    is_used = slots < tile_count[0]
    row = (owner // 8) * ROWT_DEV + tile_row
    key = jnp.where(is_used, index_of(row // COLORS, row % COLORS, Y_STRIDES), 2 * HALF)
    xs = index_of((tile_col // COLORS) * 8 + owner % 8, tile_col % COLORS, X_STRIDES)
    before = (key[None, :] < key[:, None]) | ((key[None, :] == key[:, None]) & (slots[None, :] < slots[:, None]))
    rank = jnp.sum(before.astype(jnp.int32), axis=1)
    is_here = (rank[None, :] == slots[:, None]).astype(jnp.int32)
    order = jnp.sum(is_here * slots[None, :], axis=1)
    xs = jnp.sum(is_here * xs[None, :], axis=1)
    keys = jnp.sum(is_here * key[None, :], axis=1)
    first = (keys != jnp.concatenate([jnp.full((1,), -1, jnp.int32), keys[:-1]])).astype(jnp.int32)
    rows = jnp.arange(2 * HALF, dtype=jnp.int32)
    upto = jnp.sum((key[None, :] <= rows[:, None]).astype(jnp.int32), axis=1)
    has = jnp.any(key[None, :] == rows[:, None], axis=1)
    last = jnp.where(has, upto - 1, SLOTS)

    smem = pl.BlockSpec(memory_space=pltpu.SMEM)
    vmem = pl.BlockSpec(memory_space=pltpu.VMEM)
    f32 = jnp.float32
    dma = pltpu.SemaphoreType.DMA
    flux, cond = pl.pallas_call(
        kernel,
        out_shape=(
            jax.ShapeDtypeStruct((TEMPS, COLORS * TILE), f32),
            jax.ShapeDtypeStruct((8, TILE), f32),
        ),
        in_specs=[smem] * 4 + [pl.BlockSpec(memory_space=pl.ANY)] + [vmem] * 3,
        out_specs=(vmem, vmem),
        scratch_shapes=[
            pltpu.VMEM((SLOTS, TILE, TILE), f32),
            pltpu.VMEM((SLOTS, TILE, TILE), jnp.bfloat16),
            pltpu.VMEM((SLOTS, TILE, TILE), jnp.bfloat16),
            pltpu.VMEM((2 * HALF, TEMPS, TILE), f32),
            pltpu.VMEM((SLOTS + 1, TEMPS, TILE), f32),
            pltpu.VMEM((HALF, TEMPS, TILE), f32),
            pltpu.VMEM((HALF, TEMPS, TILE), f32),
            pltpu.VMEM((HALF, TEMPS, TILE), f32),
            pltpu.VMEM((COLORS * RING_TILES, TEMPS, TILE), f32),
            pltpu.VMEM((16, 8, TILE), f32),
            dma,
            dma((COLORS, 3)),
            dma((COLORS, 3)),
            dma((COLORS, 2, 2)),
            dma((COLORS, 2, 2)),
            dma((COLORS, 4, 2, 2)),
            dma((COLORS, 4, 2, 2)),
            dma((COLORS, 13)),
            dma((COLORS, 13)),
            dma((COLORS, 4)),
            dma((COLORS, 4)),
            dma((COLORS, 4, 2, 2)),
            dma((COLORS, 4, 2, 2)),
            dma((COLORS, 2, 2)),
            dma((COLORS, 2, 2)),
            dma((COLORS, 3)),
            dma((COLORS, 3)),
            dma((3, 7)),
            dma((3, 7)),
        ],
        compiler_params=pltpu.CompilerParams(
            collective_id=0, has_side_effects=True, vmem_limit_bytes=67043328
        ),
        name="solve",
    )(
        order,
        xs,
        first,
        last,
        tile_values,
        driving.T,
        relaxation.reshape(1, COLORS * TILE),
        heat_weight.reshape(1, COLORS * TILE),
    )
    return flux.T, cond[0, :TEMPS] / cond[0, TEMPS]


def solution(mesh):
    torus = Mesh(mesh.devices.reshape(4, 4, 4, 2), AXES)
    placed = (
        P(AXES, None, None),
        P(AXES, None),
        P(AXES),
        P(AXES),
        P(AXES),
        P(AXES),
        P(AXES, None),
        P(AXES),
    )
    return jax.shard_map(
        shards, mesh=torus, in_specs=placed, out_specs=(P(AXES, None), P()), check_vma=False
    )
```

```python
import jax
import jax.numpy as jnp
from jax import lax
from jax.experimental import pallas as pl
from jax.experimental.pallas import tpu as pltpu
from jax.sharding import Mesh
from jax.sharding import PartitionSpec as P

ITERS = 3
TILE = 128
TEMPS = 64
ROWT_DEV = 24
SLOTS = 128
RING = 4
CHIPS = 64
COLORS = 3
HALF = COLORS * CHIPS
AXES = ("z", "y", "x", "core")
ORDERS = (("x", "y", "z"), ("y", "z", "x"), ("z", "x", "y"))
GROUPS = (2, 1, 3, 0)
RING_TILES = 63
NT = (((1,), (1,)), ((), ()))
NN = (((1,), (0,)), ((), ()))
STEPS = (1, 3, 2)
PARTS = 4
MESH = pl.DeviceIdType.MESH


def place(coords, color, strides):
    order = ORDERS[color]
    return coords[order[0]] + strides[0] * coords[order[1]] + strides[1] * coords[order[2]]


X_STRIDES = (4, 16)
Y_STRIDES = (16, 4)


def kernel(
    order_ref,
    xs_ref,
    first_ref,
    hr_index_ref,
    last_ref,
    tiles_hbm,
    driving_ref,
    relax_ref,
    heat_ref,
    flux_ref,
    cond_ref,
    stage,
    t_both,
    x_all,
    sums,
    y_own,
    y_pair,
    r_pair,
    r_ring,
    hr_all,
    part_ref,
    c_all,
    stage_sem,
    g1_send,
    g1_recv,
    g2_send,
    g2_recv,
    g3_send,
    g3_recv,
    fw_send,
    fw_recv,
    pr_send,
    pr_recv,
    s3_send,
    s3_recv,
    s2_send,
    s2_recv,
    s1_send,
    s1_recv,
    h_send,
    h_recv,
    c_send,
    c_recv,
):
    coords = {a: lax.axis_index(a) for a in AXES}
    core = coords["core"]
    mate = {"core": 1 - core}

    def at(axis, step):
        return {axis: lax.rem(coords[axis] + step, RING)}

    def chip_row(k):
        spot = lax.rem(coords["x"] * 2 + core + k, 8)
        return {"x": spot // 2, "core": lax.rem(spot, 2)}

    peers = [at(axis, step) for axis in ("y", "z") for step in (1, 2, 3)]
    peers += [chip_row(k) for k in range(1, 8)]
    barrier = pltpu.get_barrier_semaphore()
    for peer in peers:
        pl.semaphore_signal(barrier, inc=1, device_id=peer, device_id_type=MESH)
    load = pltpu.make_async_copy(tiles_hbm, stage, stage_sem)
    load.start()

    def lanes(c):
        return slice(c * TILE, (c + 1) * TILE)

    def relax(c):
        return relax_ref[lanes(c)].reshape(1, TILE)

    def heat(c):
        return heat_ref[lanes(c)].reshape(1, TILE)

    h_base = core * HALF
    h_own = h_base + place(coords, 0, X_STRIDES) * COLORS

    own = [(c * 2 + core) * CHIPS + place(coords, c, X_STRIDES) for c in range(COLORS)]
    for c in range(COLORS):
        x_all[own[c]] = relax(c) * driving_ref[:, lanes(c)]
        hr_all[h_own + c] = heat(c) * relax(c)
    sums[SLOTS] = jnp.zeros((TEMPS, TILE), jnp.float32)
    hr_all[2 * HALF] = jnp.zeros((1, TILE), jnp.float32)
    pl.semaphore_wait(barrier, len(peers))

    def along(c, p, step):
        return lax.rem(coords[ORDERS[c][p]] + step, RING)

    sends = []

    def plain(src, dst, ssem, rsem, device):
        return pltpu.make_async_remote_copy(
            src_ref=src, dst_ref=dst, send_sem=ssem, recv_sem=rsem, device_id=device, device_id_type=MESH
        )

    def remote(*args):
        copy = plain(*args)
        copy.start()
        sends.append(copy)
        return copy

    def drain():
        for copy in sends:
            copy.wait_send()
        sends.clear()

    def to(c, p, way):
        return at(ORDERS[c][p], 1 + 2 * way)

    def split_tiles(part):
        if part == 0:
            load.wait()

        @pl.loop(part * SLOTS // PARTS, (part + 1) * SLOTS // PARTS)
        def _(j):
            tile = stage[order_ref[j]].T
            hi = tile.astype(jnp.bfloat16)
            t_both[j, :TILE] = hi
            t_both[j, TILE:] = (tile - hi.astype(jnp.float32)).astype(jnp.bfloat16)

    def weights(stage_of):
        axis = ("x", "y", "z")[stage_of]
        first = h_base + COLORS * (
            coords["x"] * (stage_of < 1) + coords["y"] * 4 * (stage_of < 2) + coords["z"] * 16
        )
        ref = hr_all.at[pl.ds(first, COLORS * 4**stage_of)]
        return [
            plain(ref, ref, h_send.at[stage_of, step - 1], h_recv.at[stage_of, step - 1], at(axis, step))
            for step in STEPS
        ]

    def weights_to_mate():
        ref = hr_all.at[pl.ds(h_base, HALF)]
        return [plain(ref, ref, h_send.at[3, 0], h_recv.at[3, 0], mate)]

    def start(copies):
        for copy in copies:
            copy.start()

    def receive(copies):
        for copy in copies:
            copy.wait_recv()

    def first_only(sweep, *acts):
        @pl.when(sweep == 0)
        def _():
            for act in acts:
                act()

    everyone = range(COLORS)
    ways = (0, 1)

    def gather(sweep):
        near, far, wide, forwards = {}, {}, {}, []
        wide2 = {}

        def xt(c, j, g):
            return (c * 2 + core) * CHIPS + along(c, 2, j) * 16 + along(c, 1, g) * 4

        def tiles(first, count):
            return x_all.at[pl.ds(first, count)]

        def forward(c, piece, first, count):
            ref = tiles(first, count)
            forwards.append(remote(ref, ref, fw_send.at[c, piece], fw_recv.at[c, piece], mate))

        def block(c, g):
            for w in ways:
                ref = tiles(xt(c, 0, g), 4)
                wide[c, g, w] = remote(ref, ref, g3_send.at[c, g, w, 0], g3_recv.at[c, g, w, 0], to(c, 2, w))

        def relay(c, g):
            for w in ways:
                wide[c, g, w].wait_recv()
                ref = tiles(xt(c, 3 - 2 * w, g) + 2 * w, 2)
                wide2[c, g, w] = remote(ref, ref, g3_send.at[c, g, w, 1], g3_recv.at[c, g, w, 1], to(c, 2, w))
            for w in ways:
                forward(c, 1 + g * 3 + w, xt(c, 3 - 2 * w, g), 4)

        def arrived(c, g):
            for w in ways:
                wide2[c, g, w].wait_recv()
            forward(c, 3 + g * 3, xt(c, 2, g), 4)

        for c in everyone:
            for step in (1, 3, 2):
                ref = tiles(own[c], 1)
                near[c, step] = remote(
                    ref, ref, g1_send.at[c, step - 1], g1_recv.at[c, step - 1], at(ORDERS[c][0], step)
                )
        for c in everyone:
            for step in (1, 3, 2):
                near[c, step].wait_recv()
            for w in ways:
                ref = tiles(xt(c, 0, 0), 4)
                far[c, w] = remote(ref, ref, g2_send.at[c, w, 0], g2_recv.at[c, w, 0], to(c, 1, w))
        for c in everyone:
            block(c, 0)
        first_only(sweep, lambda: receive(weights(0)), lambda: start(weights(1)), lambda: split_tiles(0))
        for c in everyone:
            for w in ways:
                far[c, w].wait_recv()
                ref = tiles(xt(c, 0, 3 - 2 * w) + 2 * w, 2)
                far[c, w] = remote(ref, ref, g2_send.at[c, w, 1], g2_recv.at[c, w, 1], to(c, 1, w))
        for g in (3, 1):
            for c in everyone:
                block(c, g)
        first_only(sweep, lambda: receive(weights(1)), lambda: start(weights(2)), lambda: split_tiles(1))
        for c in everyone:
            relay(c, 0)
        for c in everyone:
            for w in ways:
                far[c, w].wait_recv()
            block(c, 2)
            forward(c, 0, (c * 2 + core) * CHIPS + along(c, 2, 0) * 16, 16)
        first_only(sweep, lambda: receive(weights(2)), lambda: start(weights_to_mate()), lambda: split_tiles(2))
        for g in (3, 1):
            for c in everyone:
                relay(c, g)
        for c in everyone:
            arrived(c, 0)
        for c in everyone:
            relay(c, 2)
        first_only(sweep, lambda: split_tiles(3))
        for g in (3, 1, 2):
            for c in everyone:
                arrived(c, g)
        first_only(sweep, lambda: receive(weights_to_mate()))
        for copy in forwards:
            copy.wait_recv()
        drain()

    def multiply():
        unroll = 8

        def some(g, carry):
            acc, part = carry
            for u in range(unroll):
                j = g * unroll + u
                x = x_all[xs_ref[j]]
                hi = x.astype(jnp.bfloat16)
                lo = (x - hi.astype(jnp.float32)).astype(jnp.bfloat16)
                prod = lax.dot_general(
                    jnp.concatenate([hi, hi], axis=1), t_both[j], NN, preferred_element_type=jnp.float32
                ) + lax.dot_general(lo, t_both[j, :TILE], NN, preferred_element_type=jnp.float32)
                acc = jnp.where(first_ref[j] != 0, 0.0, acc) + prod
                part = part + prod * hr_all[hr_index_ref[j]]
                sums[j] = acc
            return acc, part

        zero = jnp.zeros((TEMPS, TILE), jnp.float32)
        part_ref[...] = lax.fori_loop(0, SLOTS // unroll, some, (zero, zero))[1]

    row = [chip_row(k) for k in range(8)]
    rounds = (
        (0, 8, coords["x"] * 2 + core, row[1:]),
        (8, RING, coords["y"], [at("y", k) for k in (1, 2, 3)]),
        (12, RING, coords["z"], [at("z", k) for k in (1, 2, 3)]),
    )

    def totals(k):
        base, _, here, others = rounds[k]
        ref = c_all.at[base + here]
        return [plain(ref, ref, c_send.at[k, i], c_recv.at[k, i], peer) for i, peer in enumerate(others)]

    def first_total():
        part, weight = part_ref[...], 0.0
        for c in range(COLORS):
            part = part + heat(c) * relax(c) * driving_ref[:, lanes(c)]
            weight = weight + heat(c)
        ones = jnp.ones((8, TILE), jnp.float32)

        def lane_sum(rows):
            return lax.dot_general(
                ones, rows, NT, precision=lax.Precision.HIGHEST, preferred_element_type=jnp.float32
            )

        over = lane_sum(jnp.concatenate([part, part], axis=0))
        under = lane_sum(jnp.broadcast_to(weight, (TILE, TILE)))
        upper = lax.broadcasted_iota(jnp.int32, (8, TILE), 0) < 4
        return jnp.where(upper, over, under)

    def round_total(k):
        base, size = rounds[k][:2]
        receive(totals(k))
        total = c_all[base]
        for i in range(1, size):
            total = total + c_all[base + i]
        return total

    def start_round(k):
        c_all[rounds[k][0] + rounds[k][2]] = first_total() if k == 0 else round_total(k - 1)
        start(totals(k))

    def last_only(sweep, act):
        pl.when(sweep == ITERS - 1)(act)

    def scatter(sweep):
        pair, half, full = {}, {}, {}

        def yt(c, g, j):
            return c * CHIPS + along(c, 1, g) * 16 + along(c, 2, j) * 4

        def rt(c, g):
            return c * RING_TILES + g * 12

        def give(c, g):
            first = along(c, 1, g) * 16

            @pl.loop(0, 4)
            def _(q):
                for u in range(4):
                    k = first + q * 4 + u
                    y_pair[c * CHIPS + k] = sums[last_ref[(c * 2 + 1 - core) * CHIPS + k]]

            span = pl.ds(c * CHIPS + first, 16)
            pair[c, g] = remote(y_pair.at[span], r_pair.at[span], pr_send.at[c, g], pr_recv.at[c, g], mate)

        def take(c, g):
            first = along(c, 1, g) * 16
            pair[c, g].wait_recv()

            @pl.loop(0, 4)
            def _(q):
                for u in range(4):
                    k = first + q * 4 + u
                    y_own[c * CHIPS + k] = sums[last_ref[(c * 2 + core) * CHIPS + k]] + r_pair[c * CHIPS + k]

            for w in ways:
                half[c, g, w] = remote(
                    y_own.at[pl.ds(yt(c, g, 2) + 2 * w, 2)],
                    r_ring.at[pl.ds(rt(c, g) + 2 * w, 2)],
                    s3_send.at[c, g, w, 0],
                    s3_recv.at[c, g, w, 0],
                    to(c, 2, w),
                )

        def pass_on(c, g):
            for w in ways:
                half[c, g, w].wait_recv()
                near = yt(c, g, 1 + 2 * w)
                for u in range(2 * w, 2 * w + 2):
                    y_own[near + u] = y_own[near + u] + r_ring[rt(c, g) + u]
                full[c, g, w] = remote(
                    y_own.at[pl.ds(near, 4)],
                    r_ring.at[pl.ds(rt(c, g) + 4 + 4 * w, 4)],
                    s3_send.at[c, g, w, 1],
                    s3_recv.at[c, g, w, 1],
                    to(c, 2, w),
                )

        def settle(c, g):
            for w in ways:
                full[c, g, w].wait_recv()
            here = yt(c, g, 0)
            for u in range(4):
                y_own[here + u] = y_own[here + u] + (r_ring[rt(c, g) + 4 + u] + r_ring[rt(c, g) + 8 + u])

        def take2(c):
            for w in ways:
                half[c, w] = remote(
                    y_own.at[pl.ds(yt(c, 2, 0) + 2 * w, 2)],
                    r_ring.at[pl.ds(rt(c, 4) + 2 * w, 2)],
                    s2_send.at[c, w, 0],
                    s2_recv.at[c, w, 0],
                    to(c, 1, w),
                )

        def pass_on2(c):
            for w in ways:
                half[c, w].wait_recv()
                near = yt(c, 1 + 2 * w, 0)
                for u in range(2 * w, 2 * w + 2):
                    y_own[near + u] = y_own[near + u] + r_ring[rt(c, 4) + u]
                full[c, w] = remote(
                    y_own.at[pl.ds(near, 4)],
                    r_ring.at[pl.ds(rt(c, 4) + 4 + 4 * w, 4)],
                    s2_send.at[c, w, 1],
                    s2_recv.at[c, w, 1],
                    to(c, 1, w),
                )

        def settle2(c):
            for w in ways:
                full[c, w].wait_recv()
            here = yt(c, 0, 0)
            for u in range(4):
                y_own[here + u] = y_own[here + u] + (r_ring[rt(c, 4) + 4 + u] + r_ring[rt(c, 4) + 8 + u])

        for g in GROUPS:
            for c in everyone:
                give(c, g)
        plan = (
            (take, 2),
            (take, 1),
            (pass_on, 2),
            (take, 3),
            (pass_on, 1),
            (take, 0),
            (settle, 2),
            (take2,),
            (pass_on, 3),
            (pass_on, 0),
            (settle, 1),
            (settle, 3),
            (pass_on2,),
            (settle, 0),
            (settle2,),
        )
        for k, (act, *group) in enumerate(plan):
            for c in everyone:
                act(c, *group)
            if k in (1, 4, 8):
                last_only(sweep, lambda k=k: start_round((1, 4, 8).index(k)))
        last = {}
        for c in everyone:
            for step in (1, 3, 2):
                last[c, step] = remote(
                    y_own.at[pl.ds(yt(c, 0, 0) + along(c, 0, step), 1)],
                    r_ring.at[pl.ds(rt(c, 5) + step - 1, 1)],
                    s1_send.at[c, step - 1],
                    s1_recv.at[c, step - 1],
                    at(ORDERS[c][0], step),
                )
        for c in everyone:
            for step in (1, 3, 2):
                last[c, step].wait_recv()
            got = (r_ring[rt(c, 5)] + r_ring[rt(c, 5) + 1]) + r_ring[rt(c, 5) + 2]
            total = y_own[yt(c, 0, 0) + along(c, 0, 0)] + got
            flux = relax(c) * (driving_ref[:, lanes(c)] + total)
            flux_ref[:, lanes(c)] = flux
            x_all[own[c]] = flux
        drain()

    def sweep_once(sweep, carry):
        gather(sweep)
        multiply()
        scatter(sweep)
        return carry

    start(weights(0))
    lax.fori_loop(0, ITERS, sweep_once, 0)

    total = round_total(2)
    cond_ref[...] = total[0:1] / total[4:5]
    for k in range(3):
        for copy in totals(k) + weights(k):
            copy.wait_send()
    weights_to_mate()[0].wait_send()


def index_of(device, color, strides):
    coords = {"z": device // 32, "y": device // 8 % 4, "x": device // 2 % 4}
    spots = [place(coords, c, strides) for c in range(COLORS)]
    spot = jnp.where(color == 0, spots[0], jnp.where(color == 1, spots[1], spots[2]))
    return (color * 2 + device % 2) * CHIPS + spot


def shards(tile_values, tile_owner, tile_row, tile_col, tile_count, relaxation, driving, heat_weight):
    owner = tile_owner[:, 0]
    slots = jnp.arange(SLOTS, dtype=jnp.int32)
    is_used = slots < tile_count[0]
    row = (owner // 8) * ROWT_DEV + tile_row
    key = jnp.where(is_used, index_of(row // COLORS, row % COLORS, Y_STRIDES), 2 * HALF)
    xs = index_of((tile_col // COLORS) * 8 + owner % 8, tile_col % COLORS, X_STRIDES)
    before = (key[None, :] < key[:, None]) | ((key[None, :] == key[:, None]) & (slots[None, :] < slots[:, None]))
    rank = jnp.sum(before.astype(jnp.int32), axis=1)
    is_here = (rank[None, :] == slots[:, None]).astype(jnp.int32)
    order = jnp.sum(is_here * slots[None, :], axis=1)
    xs = jnp.sum(is_here * xs[None, :], axis=1)
    keys = jnp.sum(is_here * key[None, :], axis=1)
    device, color = row // COLORS, row % COLORS
    spot = {"z": device // 32, "y": device // 8 % 4, "x": device // 2 % 4}
    hr_index = (device % 2 * CHIPS + place(spot, 0, X_STRIDES)) * COLORS + color
    hr_index = jnp.sum(is_here * jnp.where(is_used, hr_index, 2 * HALF)[None, :], axis=1)
    first = (keys != jnp.concatenate([jnp.full((1,), -1, jnp.int32), keys[:-1]])).astype(jnp.int32)
    rows = jnp.arange(2 * HALF, dtype=jnp.int32)
    upto = jnp.sum((key[None, :] <= rows[:, None]).astype(jnp.int32), axis=1)
    has = jnp.any(key[None, :] == rows[:, None], axis=1)
    last = jnp.where(has, upto - 1, SLOTS)

    smem = pl.BlockSpec(memory_space=pltpu.SMEM)
    vmem = pl.BlockSpec(memory_space=pltpu.VMEM)
    f32 = jnp.float32
    dma = pltpu.SemaphoreType.DMA
    flux, cond = pl.pallas_call(
        kernel,
        out_shape=(
            jax.ShapeDtypeStruct((TEMPS, COLORS * TILE), f32),
            jax.ShapeDtypeStruct((1, TILE), f32),
        ),
        in_specs=[smem] * 5 + [pl.BlockSpec(memory_space=pl.ANY)] + [vmem] * 3,
        out_specs=(vmem, vmem),
        scratch_shapes=[
            pltpu.VMEM((SLOTS, TILE, TILE), f32),
            pltpu.VMEM((SLOTS, 2 * TILE, TILE), jnp.bfloat16),
            pltpu.VMEM((2 * HALF, TEMPS, TILE), f32),
            pltpu.VMEM((SLOTS + 1, TEMPS, TILE), f32),
            pltpu.VMEM((HALF, TEMPS, TILE), f32),
            pltpu.VMEM((HALF, TEMPS, TILE), f32),
            pltpu.VMEM((HALF, TEMPS, TILE), f32),
            pltpu.VMEM((COLORS * RING_TILES, TEMPS, TILE), f32),
            pltpu.VMEM((2 * HALF + 1, 1, TILE), f32),
            pltpu.VMEM((TEMPS, TILE), f32),
            pltpu.VMEM((16, 8, TILE), f32),
            dma,
            dma((COLORS, 3)),
            dma((COLORS, 3)),
            dma((COLORS, 2, 2)),
            dma((COLORS, 2, 2)),
            dma((COLORS, 4, 2, 2)),
            dma((COLORS, 4, 2, 2)),
            dma((COLORS, 13)),
            dma((COLORS, 13)),
            dma((COLORS, 4)),
            dma((COLORS, 4)),
            dma((COLORS, 4, 2, 2)),
            dma((COLORS, 4, 2, 2)),
            dma((COLORS, 2, 2)),
            dma((COLORS, 2, 2)),
            dma((COLORS, 3)),
            dma((COLORS, 3)),
            dma((4, 3)),
            dma((4, 3)),
            dma((3, 7)),
            dma((3, 7)),
        ],
        compiler_params=pltpu.CompilerParams(
            collective_id=0, has_side_effects=True, vmem_limit_bytes=67043328
        ),
        name="solve",
    )(
        order,
        xs,
        first,
        hr_index,
        last,
        tile_values,
        driving.T,
        relaxation,
        heat_weight,
    )
    return flux.T, cond[0, :TEMPS]


def solution(mesh):
    torus = Mesh(mesh.devices.reshape(4, 4, 4, 2), AXES)
    placed = (
        P(AXES, None, None),
        P(AXES, None),
        P(AXES),
        P(AXES),
        P(AXES),
        P(AXES),
        P(AXES, None),
        P(AXES),
    )
    return jax.shard_map(
        shards, mesh=torus, in_specs=placed, out_specs=(P(AXES, None), P()), check_vma=False
    )
```

```python
import jax
import jax.numpy as jnp
from jax import lax
from jax.experimental import pallas as pl
from jax.experimental.pallas import tpu as pltpu
from jax.sharding import Mesh
from jax.sharding import PartitionSpec as P

ITERS = 3
TILE = 128
TEMPS = 64
ROWT_DEV = 24
SLOTS = 128
RING = 4
CHIPS = 64
COLORS = 3
HALF = COLORS * CHIPS
AXES = ("z", "y", "x", "core")
ORDERS = (("x", "y", "z"), ("y", "z", "x"), ("z", "x", "y"))
GROUPS = (2, 1, 3, 0)
RING_TILES = 63
NT = (((1,), (1,)), ((), ()))
NN = (((1,), (0,)), ((), ()))
STEPS = (1, 3, 2)
PARTS = 4
MESH = pl.DeviceIdType.MESH


def place(coords, color, strides):
    order = ORDERS[color]
    return coords[order[0]] + strides[0] * coords[order[1]] + strides[1] * coords[order[2]]


X_STRIDES = (4, 16)
Y_STRIDES = (16, 4)


def kernel(
    order_ref,
    xs_ref,
    first_ref,
    hr_index_ref,
    last_ref,
    tiles_hbm,
    driving_ref,
    relax_ref,
    heat_ref,
    flux_ref,
    cond_ref,
    stage,
    t_both,
    x_all,
    sums,
    y_own,
    y_pair,
    r_pair,
    r_ring,
    hr_all,
    part_ref,
    c_all,
    stage_sem,
    g1_send,
    g1_recv,
    g2_send,
    g2_recv,
    g3_send,
    g3_recv,
    fw_send,
    fw_recv,
    pr_send,
    pr_recv,
    s3_send,
    s3_recv,
    s2_send,
    s2_recv,
    s1_send,
    s1_recv,
    h_send,
    h_recv,
    c_send,
    c_recv,
):
    coords = {a: lax.axis_index(a) for a in AXES}
    core = coords["core"]
    mate = {"core": 1 - core}

    def at(axis, step):
        return {axis: lax.rem(coords[axis] + step, RING)}

    def chip_row(k):
        spot = lax.rem(coords["x"] * 2 + core + k, 8)
        return {"x": spot // 2, "core": lax.rem(spot, 2)}

    peers = [at(axis, step) for axis in ("y", "z") for step in (1, 2, 3)]
    peers += [chip_row(k) for k in range(1, 8)]
    barrier = pltpu.get_barrier_semaphore()
    for peer in peers:
        pl.semaphore_signal(barrier, inc=1, device_id=peer, device_id_type=MESH)
    load = pltpu.make_async_copy(tiles_hbm, stage, stage_sem)
    load.start()

    def lanes(c):
        return slice(c * TILE, (c + 1) * TILE)

    def relax(c):
        return relax_ref[lanes(c)].reshape(1, TILE)

    def heat(c):
        return heat_ref[lanes(c)].reshape(1, TILE)

    h_base = core * HALF
    h_own = h_base + place(coords, 0, X_STRIDES) * COLORS

    own = [(c * 2 + core) * CHIPS + place(coords, c, X_STRIDES) for c in range(COLORS)]
    for c in range(COLORS):
        x_all[own[c]] = relax(c) * driving_ref[:, lanes(c)]
        hr_all[h_own + c] = heat(c) * relax(c)
    sums[SLOTS] = jnp.zeros((TEMPS, TILE), jnp.float32)
    hr_all[2 * HALF] = jnp.zeros((1, TILE), jnp.float32)
    pl.semaphore_wait(barrier, len(peers))

    def along(c, p, step):
        return lax.rem(coords[ORDERS[c][p]] + step, RING)

    sends = []

    def plain(src, dst, ssem, rsem, device):
        return pltpu.make_async_remote_copy(
            src_ref=src, dst_ref=dst, send_sem=ssem, recv_sem=rsem, device_id=device, device_id_type=MESH
        )

    def remote(*args):
        copy = plain(*args)
        copy.start()
        sends.append(copy)
        return copy

    def drain():
        for copy in sends:
            copy.wait_send()
        sends.clear()

    def to(c, p, way):
        return at(ORDERS[c][p], 1 + 2 * way)

    def split_tiles(part):
        if part == 0:
            load.wait()

        @pl.loop(part * SLOTS // PARTS, (part + 1) * SLOTS // PARTS)
        def _(j):
            tile = stage[order_ref[j]].T
            hi = tile.astype(jnp.bfloat16)
            t_both[j, :TILE] = hi
            t_both[j, TILE:] = (tile - hi.astype(jnp.float32)).astype(jnp.bfloat16)

    def weights(stage_of):
        axis = ("x", "y", "z")[stage_of]
        first = h_base + COLORS * (
            coords["x"] * (stage_of < 1) + coords["y"] * 4 * (stage_of < 2) + coords["z"] * 16
        )
        ref = hr_all.at[pl.ds(first, COLORS * 4**stage_of)]
        return [
            plain(ref, ref, h_send.at[stage_of, step - 1], h_recv.at[stage_of, step - 1], at(axis, step))
            for step in STEPS
        ]

    def weights_to_mate():
        ref = hr_all.at[pl.ds(h_base, HALF)]
        return [plain(ref, ref, h_send.at[3, 0], h_recv.at[3, 0], mate)]

    def start(copies):
        for copy in copies:
            copy.start()

    def receive(copies):
        for copy in copies:
            copy.wait_recv()

    def first_only(sweep, *acts):
        @pl.when(sweep == 0)
        def _():
            for act in acts:
                act()

    everyone = range(COLORS)
    ways = (0, 1)

    def gather(sweep):
        near, far, wide, forwards = {}, {}, {}, []
        wide2 = {}

        def xt(c, j, g):
            return (c * 2 + core) * CHIPS + along(c, 2, j) * 16 + along(c, 1, g) * 4

        def tiles(first, count):
            return x_all.at[pl.ds(first, count)]

        def forward(c, piece, first, count):
            ref = tiles(first, count)
            forwards.append(remote(ref, ref, fw_send.at[c, piece], fw_recv.at[c, piece], mate))

        def block(c, g):
            for w in ways:
                ref = tiles(xt(c, 0, g), 4)
                wide[c, g, w] = remote(ref, ref, g3_send.at[c, g, w, 0], g3_recv.at[c, g, w, 0], to(c, 2, w))

        def relay(c, g):
            for w in ways:
                wide[c, g, w].wait_recv()
                ref = tiles(xt(c, 3 - 2 * w, g) + 2 * w, 2)
                wide2[c, g, w] = remote(ref, ref, g3_send.at[c, g, w, 1], g3_recv.at[c, g, w, 1], to(c, 2, w))
            for w in ways:
                forward(c, 1 + g * 3 + w, xt(c, 3 - 2 * w, g), 4)

        def arrived(c, g):
            for w in ways:
                wide2[c, g, w].wait_recv()
            forward(c, 3 + g * 3, xt(c, 2, g), 4)

        for c in everyone:
            for step in (1, 3, 2):
                ref = tiles(own[c], 1)
                near[c, step] = remote(
                    ref, ref, g1_send.at[c, step - 1], g1_recv.at[c, step - 1], at(ORDERS[c][0], step)
                )
        for c in everyone:
            for step in (1, 3, 2):
                near[c, step].wait_recv()
            for w in ways:
                ref = tiles(xt(c, 0, 0), 4)
                far[c, w] = remote(ref, ref, g2_send.at[c, w, 0], g2_recv.at[c, w, 0], to(c, 1, w))
        for c in everyone:
            block(c, 0)
        first_only(sweep, lambda: receive(weights(0)), lambda: start(weights(1)), lambda: split_tiles(0))
        for c in everyone:
            for w in ways:
                far[c, w].wait_recv()
                ref = tiles(xt(c, 0, 3 - 2 * w) + 2 * w, 2)
                far[c, w] = remote(ref, ref, g2_send.at[c, w, 1], g2_recv.at[c, w, 1], to(c, 1, w))
        for g in (3, 1):
            for c in everyone:
                block(c, g)
        first_only(sweep, lambda: receive(weights(1)), lambda: start(weights(2)), lambda: split_tiles(1))
        for c in everyone:
            relay(c, 0)
        for c in everyone:
            for w in ways:
                far[c, w].wait_recv()
            block(c, 2)
            forward(c, 0, (c * 2 + core) * CHIPS + along(c, 2, 0) * 16, 16)
        first_only(sweep, lambda: receive(weights(2)), lambda: start(weights_to_mate()), lambda: split_tiles(2))
        for g in (3, 1):
            for c in everyone:
                relay(c, g)
        for c in everyone:
            arrived(c, 0)
        for c in everyone:
            relay(c, 2)
        first_only(sweep, lambda: split_tiles(3))
        for g in (3, 1, 2):
            for c in everyone:
                arrived(c, g)
        first_only(sweep, lambda: receive(weights_to_mate()))
        for copy in forwards:
            copy.wait_recv()
        drain()

    def multiply():
        unroll = 8

        def some(g, carry):
            acc, part = carry
            for u in range(unroll):
                j = g * unroll + u
                x = x_all[xs_ref[j]]
                hi = x.astype(jnp.bfloat16)
                lo = (x - hi.astype(jnp.float32)).astype(jnp.bfloat16)
                prod = lax.dot_general(
                    jnp.concatenate([hi, hi], axis=1), t_both[j], NN, preferred_element_type=jnp.float32
                ) + lax.dot_general(lo, t_both[j, :TILE], NN, preferred_element_type=jnp.float32)
                acc = jnp.where(first_ref[j] != 0, 0.0, acc) + prod
                part = part + prod * hr_all[hr_index_ref[j]]
                sums[j] = acc
            return acc, part

        zero = jnp.zeros((TEMPS, TILE), jnp.float32)
        part_ref[...] = lax.fori_loop(0, SLOTS // unroll, some, (zero, zero))[1]

    row = [chip_row(k) for k in range(8)]
    rounds = (
        (0, 8, coords["x"] * 2 + core, row[1:]),
        (8, RING, coords["y"], [at("y", k) for k in (1, 2, 3)]),
        (12, RING, coords["z"], [at("z", k) for k in (1, 2, 3)]),
    )

    def totals(k):
        base, _, here, others = rounds[k]
        ref = c_all.at[base + here]
        return [plain(ref, ref, c_send.at[k, i], c_recv.at[k, i], peer) for i, peer in enumerate(others)]

    def first_total():
        part, weight = part_ref[...], 0.0
        for c in range(COLORS):
            part = part + heat(c) * relax(c) * driving_ref[:, lanes(c)]
            weight = weight + heat(c)
        ones = jnp.ones((8, TILE), jnp.float32)

        def lane_sum(rows):
            return lax.dot_general(
                ones, rows, NT, precision=lax.Precision.HIGHEST, preferred_element_type=jnp.float32
            )

        over = lane_sum(jnp.concatenate([part, part], axis=0))
        under = lane_sum(jnp.broadcast_to(weight, (TILE, TILE)))
        upper = lax.broadcasted_iota(jnp.int32, (8, TILE), 0) < 4
        return jnp.where(upper, over, under)

    def round_total(k):
        base, size = rounds[k][:2]
        receive(totals(k))
        total = c_all[base]
        for i in range(1, size):
            total = total + c_all[base + i]
        return total

    def start_round(k):
        c_all[rounds[k][0] + rounds[k][2]] = first_total() if k == 0 else round_total(k - 1)
        start(totals(k))

    def last_only(sweep, act):
        pl.when(sweep == ITERS - 1)(act)

    def scatter(sweep):
        pair, half, full = {}, {}, {}

        def yt(c, g, j):
            return c * CHIPS + along(c, 1, g) * 16 + along(c, 2, j) * 4

        def rt(c, g):
            return c * RING_TILES + g * 12

        def give(c, g, j):
            first = yt(c, g, j)
            for u in range(4):
                y_pair[first + u] = sums[last_ref[c * CHIPS + (1 - core) * CHIPS + first + u]]
            span = pl.ds(first, 4)
            pair[c, g, j] = remote(y_pair.at[span], r_pair.at[span], pr_send.at[c, g, j], pr_recv.at[c, g, j], mate)

        def both_cores(c, g, j):
            first = yt(c, g, j)
            pair[c, g, j].wait_recv()
            return first, [
                sums[last_ref[c * CHIPS + core * CHIPS + first + u]] + r_pair[first + u] for u in range(4)
            ]

        def take(c, g):
            first, rows = both_cores(c, g, 2)
            for u in range(4):
                y_own[first + u] = rows[u]
            for w in ways:
                half[c, g, w] = remote(
                    y_own.at[pl.ds(first + 2 * w, 2)],
                    r_ring.at[pl.ds(rt(c, g) + 2 * w, 2)],
                    s3_send.at[c, g, w, 0],
                    s3_recv.at[c, g, w, 0],
                    to(c, 2, w),
                )

        def pass_on(c, g):
            for w in ways:
                near, rows = both_cores(c, g, 1 + 2 * w)
                half[c, g, w].wait_recv()
                for u in range(4):
                    y_own[near + u] = rows[u] + r_ring[rt(c, g) + u] if u // 2 == w else rows[u]
                full[c, g, w] = remote(
                    y_own.at[pl.ds(near, 4)],
                    r_ring.at[pl.ds(rt(c, g) + 4 + 4 * w, 4)],
                    s3_send.at[c, g, w, 1],
                    s3_recv.at[c, g, w, 1],
                    to(c, 2, w),
                )

        def settle(c, g):
            here, rows = both_cores(c, g, 0)
            for w in ways:
                full[c, g, w].wait_recv()
            for u in range(4):
                y_own[here + u] = rows[u] + (r_ring[rt(c, g) + 4 + u] + r_ring[rt(c, g) + 8 + u])

        def take2(c):
            for w in ways:
                half[c, w] = remote(
                    y_own.at[pl.ds(yt(c, 2, 0) + 2 * w, 2)],
                    r_ring.at[pl.ds(rt(c, 4) + 2 * w, 2)],
                    s2_send.at[c, w, 0],
                    s2_recv.at[c, w, 0],
                    to(c, 1, w),
                )

        def pass_on2(c):
            for w in ways:
                half[c, w].wait_recv()
                near = yt(c, 1 + 2 * w, 0)
                for u in range(2 * w, 2 * w + 2):
                    y_own[near + u] = y_own[near + u] + r_ring[rt(c, 4) + u]
                full[c, w] = remote(
                    y_own.at[pl.ds(near, 4)],
                    r_ring.at[pl.ds(rt(c, 4) + 4 + 4 * w, 4)],
                    s2_send.at[c, w, 1],
                    s2_recv.at[c, w, 1],
                    to(c, 1, w),
                )

        def settle2(c):
            for w in ways:
                full[c, w].wait_recv()
            here = yt(c, 0, 0)
            for u in range(4):
                y_own[here + u] = y_own[here + u] + (r_ring[rt(c, 4) + 4 + u] + r_ring[rt(c, 4) + 8 + u])

        for j, groups in ((2, GROUPS), (1, (2,)), (3, (2,)), (1, (1,)), (3, (1,)), (1, (3,)), (3, (3,))):
            for g in groups:
                for c in everyone:
                    give(c, g, j)
        for j, groups in ((0, (2,)), (1, (0,)), (3, (0,)), (0, (1, 3, 0))):
            for g in groups:
                for c in everyone:
                    give(c, g, j)
        plan = (
            (take, 2),
            (take, 1),
            (take, 3),
            (take, 0),
            (pass_on, 2),
            (pass_on, 1),
            (pass_on, 3),
            (settle, 2),
            (take2,),
            (pass_on, 0),
            (settle, 1),
            (settle, 3),
            (pass_on2,),
            (settle, 0),
            (settle2,),
        )
        for k, (act, *group) in enumerate(plan):
            for c in everyone:
                act(c, *group)
            if k in (3, 7, 10):
                last_only(sweep, lambda k=k: start_round((3, 7, 10).index(k)))
        last = {}
        for c in everyone:
            for step in (1, 3, 2):
                last[c, step] = remote(
                    y_own.at[pl.ds(yt(c, 0, 0) + along(c, 0, step), 1)],
                    r_ring.at[pl.ds(rt(c, 5) + step - 1, 1)],
                    s1_send.at[c, step - 1],
                    s1_recv.at[c, step - 1],
                    at(ORDERS[c][0], step),
                )
        for c in everyone:
            for step in (1, 3, 2):
                last[c, step].wait_recv()
            got = (r_ring[rt(c, 5)] + r_ring[rt(c, 5) + 1]) + r_ring[rt(c, 5) + 2]
            total = y_own[yt(c, 0, 0) + along(c, 0, 0)] + got
            flux = relax(c) * (driving_ref[:, lanes(c)] + total)
            flux_ref[:, lanes(c)] = flux
            x_all[own[c]] = flux
        drain()

    def sweep_once(sweep, carry):
        gather(sweep)
        multiply()
        scatter(sweep)
        return carry

    start(weights(0))
    lax.fori_loop(0, ITERS, sweep_once, 0)

    total = round_total(2)
    cond_ref[...] = total[0:1] / total[4:5]
    for k in range(3):
        for copy in totals(k) + weights(k):
            copy.wait_send()
    weights_to_mate()[0].wait_send()


def index_of(device, color, strides):
    coords = {"z": device // 32, "y": device // 8 % 4, "x": device // 2 % 4}
    spots = [place(coords, c, strides) for c in range(COLORS)]
    spot = jnp.where(color == 0, spots[0], jnp.where(color == 1, spots[1], spots[2]))
    return (color * 2 + device % 2) * CHIPS + spot


def shards(tile_values, tile_owner, tile_row, tile_col, tile_count, relaxation, driving, heat_weight):
    owner = tile_owner[:, 0]
    slots = jnp.arange(SLOTS, dtype=jnp.int32)
    is_used = slots < tile_count[0]
    row = (owner // 8) * ROWT_DEV + tile_row
    key = jnp.where(is_used, index_of(row // COLORS, row % COLORS, Y_STRIDES), 2 * HALF)
    xs = index_of((tile_col // COLORS) * 8 + owner % 8, tile_col % COLORS, X_STRIDES)
    before = (key[None, :] < key[:, None]) | ((key[None, :] == key[:, None]) & (slots[None, :] < slots[:, None]))
    rank = jnp.sum(before.astype(jnp.int32), axis=1)
    is_here = (rank[None, :] == slots[:, None]).astype(jnp.int32)
    order = jnp.sum(is_here * slots[None, :], axis=1)
    xs = jnp.sum(is_here * xs[None, :], axis=1)
    keys = jnp.sum(is_here * key[None, :], axis=1)
    device, color = row // COLORS, row % COLORS
    spot = {"z": device // 32, "y": device // 8 % 4, "x": device // 2 % 4}
    hr_index = (device % 2 * CHIPS + place(spot, 0, X_STRIDES)) * COLORS + color
    hr_index = jnp.sum(is_here * jnp.where(is_used, hr_index, 2 * HALF)[None, :], axis=1)
    first = (keys != jnp.concatenate([jnp.full((1,), -1, jnp.int32), keys[:-1]])).astype(jnp.int32)
    rows = jnp.arange(2 * HALF, dtype=jnp.int32)
    upto = jnp.sum((key[None, :] <= rows[:, None]).astype(jnp.int32), axis=1)
    has = jnp.any(key[None, :] == rows[:, None], axis=1)
    last = jnp.where(has, upto - 1, SLOTS)

    smem = pl.BlockSpec(memory_space=pltpu.SMEM)
    vmem = pl.BlockSpec(memory_space=pltpu.VMEM)
    f32 = jnp.float32
    dma = pltpu.SemaphoreType.DMA
    flux, cond = pl.pallas_call(
        kernel,
        out_shape=(
            jax.ShapeDtypeStruct((TEMPS, COLORS * TILE), f32),
            jax.ShapeDtypeStruct((1, TILE), f32),
        ),
        in_specs=[smem] * 5 + [pl.BlockSpec(memory_space=pl.ANY)] + [vmem] * 3,
        out_specs=(vmem, vmem),
        scratch_shapes=[
            pltpu.VMEM((SLOTS, TILE, TILE), f32),
            pltpu.VMEM((SLOTS, 2 * TILE, TILE), jnp.bfloat16),
            pltpu.VMEM((2 * HALF, TEMPS, TILE), f32),
            pltpu.VMEM((SLOTS + 1, TEMPS, TILE), f32),
            pltpu.VMEM((HALF, TEMPS, TILE), f32),
            pltpu.VMEM((HALF, TEMPS, TILE), f32),
            pltpu.VMEM((HALF, TEMPS, TILE), f32),
            pltpu.VMEM((COLORS * RING_TILES, TEMPS, TILE), f32),
            pltpu.VMEM((2 * HALF + 1, 1, TILE), f32),
            pltpu.VMEM((TEMPS, TILE), f32),
            pltpu.VMEM((16, 8, TILE), f32),
            dma,
            dma((COLORS, 3)),
            dma((COLORS, 3)),
            dma((COLORS, 2, 2)),
            dma((COLORS, 2, 2)),
            dma((COLORS, 4, 2, 2)),
            dma((COLORS, 4, 2, 2)),
            dma((COLORS, 13)),
            dma((COLORS, 13)),
            dma((COLORS, 4, 4)),
            dma((COLORS, 4, 4)),
            dma((COLORS, 4, 2, 2)),
            dma((COLORS, 4, 2, 2)),
            dma((COLORS, 2, 2)),
            dma((COLORS, 2, 2)),
            dma((COLORS, 3)),
            dma((COLORS, 3)),
            dma((4, 3)),
            dma((4, 3)),
            dma((3, 7)),
            dma((3, 7)),
        ],
        compiler_params=pltpu.CompilerParams(
            collective_id=0, has_side_effects=True, vmem_limit_bytes=67043328
        ),
        name="solve",
    )(
        order,
        xs,
        first,
        hr_index,
        last,
        tile_values,
        driving.T,
        relaxation,
        heat_weight,
    )
    return flux.T, cond[0, :TEMPS]


def solution(mesh):
    torus = Mesh(mesh.devices.reshape(4, 4, 4, 2), AXES)
    placed = (
        P(AXES, None, None),
        P(AXES, None),
        P(AXES),
        P(AXES),
        P(AXES),
        P(AXES),
        P(AXES, None),
        P(AXES),
    )
    return jax.shard_map(
        shards, mesh=torus, in_specs=placed, out_specs=(P(AXES, None), P()), check_vma=False
    )
```

```python
import jax
import jax.numpy as jnp
from jax import lax
from jax.experimental import pallas as pl
from jax.experimental.pallas import tpu as pltpu
from jax.sharding import Mesh
from jax.sharding import PartitionSpec as P

ITERS = 3
TILE = 128
TEMPS = 64
ROWT_DEV = 24
SLOTS = 128
RING = 4
CHIPS = 64
COLORS = 3
HALF = COLORS * CHIPS
AXES = ("z", "y", "x", "core")
ORDERS = (("x", "y", "z"), ("y", "z", "x"), ("z", "x", "y"))
GROUPS = (2, 1, 3, 0)
RING_TILES = 63
NT = (((1,), (1,)), ((), ()))
NN = (((1,), (0,)), ((), ()))
STEPS = (1, 3, 2)
PARTS = 4
MESH = pl.DeviceIdType.MESH


def place(coords, color, strides):
    order = ORDERS[color]
    return coords[order[0]] + strides[0] * coords[order[1]] + strides[1] * coords[order[2]]


X_STRIDES = (4, 16)
Y_STRIDES = (16, 4)


def kernel(
    order_ref,
    xs_ref,
    keys_ref,
    hr_index_ref,
    last_ref,
    tiles_hbm,
    driving_ref,
    relax_ref,
    heat_ref,
    flux_ref,
    cond_ref,
    stage,
    t_both,
    x_all,
    sums,
    y_own,
    y_pair,
    r_pair,
    r_ring,
    hr_all,
    part_ref,
    c_all,
    stage_sem,
    g1_send,
    g1_recv,
    g2_send,
    g2_recv,
    g3_send,
    g3_recv,
    fw_send,
    fw_recv,
    pr_send,
    pr_recv,
    s3_send,
    s3_recv,
    s2_send,
    s2_recv,
    s1_send,
    s1_recv,
    h_send,
    h_recv,
    c_send,
    c_recv,
):
    coords = {a: lax.axis_index(a) for a in AXES}
    core = coords["core"]
    mate = {"core": 1 - core}

    def at(axis, step):
        return {axis: lax.rem(coords[axis] + step, RING)}

    def chip_row(k):
        spot = lax.rem(coords["x"] * 2 + core + k, 8)
        return {"x": spot // 2, "core": lax.rem(spot, 2)}

    peers = [at(axis, step) for axis in ("y", "z") for step in (1, 2, 3)]
    peers += [chip_row(k) for k in range(1, 8)]
    barrier = pltpu.get_barrier_semaphore()
    for peer in peers:
        pl.semaphore_signal(barrier, inc=1, device_id=peer, device_id_type=MESH)
    load = pltpu.make_async_copy(tiles_hbm, stage, stage_sem)
    load.start()

    def lanes(c):
        return slice(c * TILE, (c + 1) * TILE)

    def relax(c):
        return relax_ref[lanes(c)].reshape(1, TILE)

    def heat(c):
        return heat_ref[lanes(c)].reshape(1, TILE)

    h_base = core * HALF
    h_own = h_base + place(coords, 0, X_STRIDES) * COLORS

    own = [(c * 2 + core) * CHIPS + place(coords, c, X_STRIDES) for c in range(COLORS)]
    for c in range(COLORS):
        x_all[own[c]] = relax(c) * driving_ref[:, lanes(c)]
        hr_all[h_own + c] = heat(c) * relax(c)
    sums[SLOTS] = jnp.zeros((TEMPS, TILE), jnp.float32)
    hr_all[2 * HALF] = jnp.zeros((1, TILE), jnp.float32)
    pl.semaphore_wait(barrier, len(peers))

    def along(c, p, step):
        return lax.rem(coords[ORDERS[c][p]] + step, RING)

    sends = []

    def plain(src, dst, ssem, rsem, device):
        return pltpu.make_async_remote_copy(
            src_ref=src, dst_ref=dst, send_sem=ssem, recv_sem=rsem, device_id=device, device_id_type=MESH
        )

    def remote(*args):
        copy = plain(*args)
        copy.start()
        sends.append(copy)
        return copy

    def drain():
        for copy in sends:
            copy.wait_send()
        sends.clear()

    def to(c, p, way):
        return at(ORDERS[c][p], 1 + 2 * way)

    def split_tiles(part):
        if part == 0:
            load.wait()

        @pl.loop(part * SLOTS // PARTS, (part + 1) * SLOTS // PARTS)
        def _(j):
            tile = stage[order_ref[j]].T
            hi = tile.astype(jnp.bfloat16)
            t_both[j, :TILE] = hi
            t_both[j, TILE:] = (tile - hi.astype(jnp.float32)).astype(jnp.bfloat16)

    def weights(stage_of):
        axis = ("x", "y", "z")[stage_of]
        first = h_base + COLORS * (
            coords["x"] * (stage_of < 1) + coords["y"] * 4 * (stage_of < 2) + coords["z"] * 16
        )
        ref = hr_all.at[pl.ds(first, COLORS * 4**stage_of)]
        return [
            plain(ref, ref, h_send.at[stage_of, step - 1], h_recv.at[stage_of, step - 1], at(axis, step))
            for step in STEPS
        ]

    def weights_to_mate():
        ref = hr_all.at[pl.ds(h_base, HALF)]
        return [plain(ref, ref, h_send.at[3, 0], h_recv.at[3, 0], mate)]

    def start(copies):
        for copy in copies:
            copy.start()

    def receive(copies):
        for copy in copies:
            copy.wait_recv()

    def first_only(sweep, *acts):
        @pl.when(sweep == 0)
        def _():
            for act in acts:
                act()

    everyone = range(COLORS)
    ways = (0, 1)

    def gather(sweep):
        near, far, wide, forwards = {}, {}, {}, []
        wide2 = {}

        def xt(c, j, g):
            return (c * 2 + core) * CHIPS + along(c, 2, j) * 16 + along(c, 1, g) * 4

        def tiles(first, count):
            return x_all.at[pl.ds(first, count)]

        def forward(c, piece, first, count):
            ref = tiles(first, count)
            forwards.append(remote(ref, ref, fw_send.at[c, piece], fw_recv.at[c, piece], mate))

        def block(c, g):
            for w in ways:
                ref = tiles(xt(c, 0, g), 4)
                wide[c, g, w] = remote(ref, ref, g3_send.at[c, g, w, 0], g3_recv.at[c, g, w, 0], to(c, 2, w))

        def relay(c, g):
            for w in ways:
                wide[c, g, w].wait_recv()
                ref = tiles(xt(c, 3 - 2 * w, g) + 2 * w, 2)
                wide2[c, g, w] = remote(ref, ref, g3_send.at[c, g, w, 1], g3_recv.at[c, g, w, 1], to(c, 2, w))
            for w in ways:
                forward(c, 1 + g * 3 + w, xt(c, 3 - 2 * w, g), 4)

        def arrived(c, g):
            for w in ways:
                wide2[c, g, w].wait_recv()
            forward(c, 3 + g * 3, xt(c, 2, g), 4)

        for c in everyone:
            for step in (1, 3, 2):
                ref = tiles(own[c], 1)
                near[c, step] = remote(
                    ref, ref, g1_send.at[c, step - 1], g1_recv.at[c, step - 1], at(ORDERS[c][0], step)
                )
        def send2(c, i, k):
            ref = tiles(xt(c, 0, 0) + along(c, 0, k), 1)
            for w in ways:
                far[c, w, i] = remote(ref, ref, g2_send.at[c, w, 1 + i], g2_recv.at[c, w, 1 + i], to(c, 1, w))

        for c in everyone:
            send2(c, 0, 0)
        for step in (1, 3, 2):
            for c in everyone:
                near[c, step].wait_recv()
                send2(c, step, 4 - step)
        for c in everyone:
            block(c, 0)
        first_only(sweep, lambda: receive(weights(0)), lambda: start(weights(1)), lambda: split_tiles(0))
        for c in everyone:
            for w in ways:
                for i in range(4):
                    far[c, w, i].wait_recv()
                ref = tiles(xt(c, 0, 3 - 2 * w) + 2 * w, 2)
                far[c, w] = remote(ref, ref, g2_send.at[c, w, 0], g2_recv.at[c, w, 0], to(c, 1, w))
        for g in (3, 1):
            for c in everyone:
                block(c, g)
        first_only(sweep, lambda: receive(weights(1)), lambda: start(weights(2)), lambda: split_tiles(1))
        for c in everyone:
            relay(c, 0)
        for c in everyone:
            for w in ways:
                far[c, w].wait_recv()
            block(c, 2)
            forward(c, 0, (c * 2 + core) * CHIPS + along(c, 2, 0) * 16, 16)
        first_only(sweep, lambda: receive(weights(2)), lambda: start(weights_to_mate()), lambda: split_tiles(2))
        for g in (3, 1):
            for c in everyone:
                relay(c, g)
        for c in everyone:
            arrived(c, 0)
        for c in everyone:
            relay(c, 2)
        first_only(sweep, lambda: split_tiles(3))
        for g in (3, 1, 2):
            for c in everyone:
                arrived(c, g)
        first_only(sweep, lambda: receive(weights_to_mate()))
        for copy in forwards:
            copy.wait_recv()
        drain()

    def multiply():
        unroll = 32

        def some(g, carry):
            acc, part = carry
            for u in range(unroll):
                j = g * unroll + u
                x = x_all[xs_ref[j]]
                hi = x.astype(jnp.bfloat16)
                lo = (x - hi.astype(jnp.float32)).astype(jnp.bfloat16)
                prod = lax.dot_general(
                    jnp.concatenate([hi, hi], axis=1), t_both[j], NN, preferred_element_type=jnp.float32
                ) + lax.dot_general(lo, t_both[j, :TILE], NN, preferred_element_type=jnp.float32)
                acc = jnp.where(keys_ref[j] != keys_ref[lax.max(j - 1, 0)], 0.0, acc) + prod
                part = part + prod * hr_all[hr_index_ref[j]]
                sums[j] = acc
            return acc, part

        zero = jnp.zeros((TEMPS, TILE), jnp.float32)
        part_ref[...] = lax.fori_loop(0, SLOTS // unroll, some, (zero, zero))[1]

    row = [chip_row(k) for k in range(8)]
    rounds = (
        (0, 8, coords["x"] * 2 + core, row[1:]),
        (8, RING, coords["y"], [at("y", k) for k in (1, 2, 3)]),
        (12, RING, coords["z"], [at("z", k) for k in (1, 2, 3)]),
    )

    def totals(k):
        base, _, here, others = rounds[k]
        ref = c_all.at[base + here]
        return [plain(ref, ref, c_send.at[k, i], c_recv.at[k, i], peer) for i, peer in enumerate(others)]

    def first_total():
        part, weight = part_ref[...], 0.0
        for c in range(COLORS):
            part = part + heat(c) * relax(c) * driving_ref[:, lanes(c)]
            weight = weight + heat(c)
        ones = jnp.ones((8, TILE), jnp.float32)

        def lane_sum(rows):
            return lax.dot_general(
                ones, rows, NT, precision=lax.Precision.HIGHEST, preferred_element_type=jnp.float32
            )

        over = lane_sum(jnp.concatenate([part, part], axis=0))
        under = lane_sum(jnp.broadcast_to(weight, (TILE, TILE)))
        upper = lax.broadcasted_iota(jnp.int32, (8, TILE), 0) < 4
        return jnp.where(upper, over, under)

    def round_total(k):
        base, size = rounds[k][:2]
        receive(totals(k))
        total = c_all[base]
        for i in range(1, size):
            total = total + c_all[base + i]
        return total

    def start_round(k):
        c_all[rounds[k][0] + rounds[k][2]] = first_total() if k == 0 else round_total(k - 1)
        start(totals(k))

    def last_only(sweep, act):
        pl.when(sweep == ITERS - 1)(act)

    def scatter(sweep):
        pair, half, full, tail, last = {}, {}, {}, {}, {}

        def yt(c, g, j):
            return c * CHIPS + along(c, 1, g) * 16 + along(c, 2, j) * 4

        def rt(c, g):
            return c * RING_TILES + g * 12

        def give(c, g, j):
            first = yt(c, g, j)
            for u in range(4):
                y_pair[first + u] = sums[last_ref[c * CHIPS + (1 - core) * CHIPS + first + u]]
            span = pl.ds(first, 4)
            pair[c, g, j] = remote(y_pair.at[span], r_pair.at[span], pr_send.at[c, g, j], pr_recv.at[c, g, j], mate)

        def both_cores(c, g, j):
            first = yt(c, g, j)
            pair[c, g, j].wait_recv()
            return first, [
                sums[last_ref[c * CHIPS + core * CHIPS + first + u]] + r_pair[first + u] for u in range(4)
            ]

        def take(c, g):
            first, rows = both_cores(c, g, 2)
            for u in range(4):
                y_own[first + u] = rows[u]
            for w in ways:
                half[c, g, w] = remote(
                    y_own.at[pl.ds(first + 2 * w, 2)],
                    r_ring.at[pl.ds(rt(c, g) + 2 * w, 2)],
                    s3_send.at[c, g, w, 0],
                    s3_recv.at[c, g, w, 0],
                    to(c, 2, w),
                )

        def pass_on(c, g):
            for w in ways:
                near, rows = both_cores(c, g, 1 + 2 * w)
                half[c, g, w].wait_recv()
                for u in range(4):
                    y_own[near + u] = rows[u] + r_ring[rt(c, g) + u] if u // 2 == w else rows[u]
                full[c, g, w] = remote(
                    y_own.at[pl.ds(near, 4)],
                    r_ring.at[pl.ds(rt(c, g) + 4 + 4 * w, 4)],
                    s3_send.at[c, g, w, 1],
                    s3_recv.at[c, g, w, 1],
                    to(c, 2, w),
                )

        def settle(c, g):
            here, rows = both_cores(c, g, 0)
            for w in ways:
                full[c, g, w].wait_recv()
            for u in range(4):
                y_own[here + u] = rows[u] + (r_ring[rt(c, g) + 4 + u] + r_ring[rt(c, g) + 8 + u])

        def take2(c):
            for w in ways:
                half[c, w] = remote(
                    y_own.at[pl.ds(yt(c, 2, 0) + 2 * w, 2)],
                    r_ring.at[pl.ds(rt(c, 4) + 2 * w, 2)],
                    s2_send.at[c, w, 0],
                    s2_recv.at[c, w, 0],
                    to(c, 1, w),
                )

        def pass_on2(c):
            for w in ways:
                half[c, w].wait_recv()
                near = yt(c, 1 + 2 * w, 0)
                for u in range(2 * w, 2 * w + 2):
                    y_own[near + u] = y_own[near + u] + r_ring[rt(c, 4) + u]
            for step in (2, 1, 3, 0):
                for w in ways:
                    k = along(c, 0, step)
                    tail[c, w, step] = remote(
                        y_own.at[pl.ds(yt(c, 1 + 2 * w, 0) + k, 1)],
                        r_ring.at[pl.ds(rt(c, 4) + 4 + 4 * w + k, 1)],
                        s2_send.at[c, w, 1 + step],
                        s2_recv.at[c, w, 1 + step],
                        to(c, 1, w),
                    )

        def settle2(c, step):
            for w in ways:
                tail[c, w, step].wait_recv()
            k = along(c, 0, step)
            here = yt(c, 0, 0) + k
            y_own[here] = y_own[here] + (r_ring[rt(c, 4) + 4 + k] + r_ring[rt(c, 4) + 8 + k])
            if step:
                last[c, step] = remote(
                    y_own.at[pl.ds(here, 1)],
                    r_ring.at[pl.ds(rt(c, 5) + step - 1, 1)],
                    s1_send.at[c, step - 1],
                    s1_recv.at[c, step - 1],
                    at(ORDERS[c][0], step),
                )

        for j, groups in ((2, GROUPS), (1, (2,)), (3, (2,)), (1, (1,)), (3, (1,)), (1, (3,)), (3, (3,))):
            for g in groups:
                for c in everyone:
                    give(c, g, j)
        for j, groups in ((0, (2,)), (1, (0,)), (3, (0,)), (0, (1, 3, 0))):
            for g in groups:
                for c in everyone:
                    give(c, g, j)
        plan = (
            (take, 2),
            (take, 1),
            (take, 3),
            (take, 0),
            (pass_on, 2),
            (pass_on, 1),
            (pass_on, 3),
            (settle, 2),
            (take2,),
            (pass_on, 0),
            (settle, 1),
            (settle, 3),
            (pass_on2,),
            (settle, 0),
            (settle2, 2),
            (settle2, 1),
            (settle2, 3),
            (settle2, 0),
        )
        for k, (act, *group) in enumerate(plan):
            for c in everyone:
                act(c, *group)
            if k in (3, 7, 10):
                last_only(sweep, lambda k=k: start_round((3, 7, 10).index(k)))
        for c in everyone:
            for step in (1, 3, 2):
                last[c, step].wait_recv()
            got = (r_ring[rt(c, 5)] + r_ring[rt(c, 5) + 1]) + r_ring[rt(c, 5) + 2]
            total = y_own[yt(c, 0, 0) + along(c, 0, 0)] + got
            flux = relax(c) * (driving_ref[:, lanes(c)] + total)
            flux_ref[:, lanes(c)] = flux
            x_all[own[c]] = flux
        drain()

    def sweep_once(sweep, carry):
        gather(sweep)
        multiply()
        scatter(sweep)
        return carry

    start(weights(0))
    lax.fori_loop(0, ITERS, sweep_once, 0)

    total = round_total(2)
    cond_ref[...] = total[0:1] / total[4:5]
    for k in range(3):
        for copy in totals(k) + weights(k):
            copy.wait_send()
    weights_to_mate()[0].wait_send()


def index_of(device, color, strides):
    coords = {"z": device // 32, "y": device // 8 % 4, "x": device // 2 % 4}
    spots = [place(coords, c, strides) for c in range(COLORS)]
    spot = jnp.where(color == 0, spots[0], jnp.where(color == 1, spots[1], spots[2]))
    return (color * 2 + device % 2) * CHIPS + spot


def shards(tile_values, tile_owner, tile_row, tile_col, tile_count, relaxation, driving, heat_weight):
    owner = tile_owner[:, 0]
    slots = jnp.arange(SLOTS, dtype=jnp.int32)
    is_used = slots < tile_count[0]
    row = (owner // 8) * ROWT_DEV + tile_row
    key = jnp.where(is_used, index_of(row // COLORS, row % COLORS, Y_STRIDES), 2 * HALF)
    xs = index_of((tile_col // COLORS) * 8 + owner % 8, tile_col % COLORS, X_STRIDES)
    before = (key[None, :] < key[:, None]) | ((key[None, :] == key[:, None]) & (slots[None, :] < slots[:, None]))
    rank = jnp.sum(before.astype(jnp.int32), axis=1)
    is_here = (rank[None, :] == slots[:, None]).astype(jnp.int32)
    order = jnp.sum(is_here * slots[None, :], axis=1)
    xs = jnp.sum(is_here * xs[None, :], axis=1)
    keys = jnp.sum(is_here * key[None, :], axis=1)
    device, color = row // COLORS, row % COLORS
    spot = {"z": device // 32, "y": device // 8 % 4, "x": device // 2 % 4}
    hr_index = (device % 2 * CHIPS + place(spot, 0, X_STRIDES)) * COLORS + color
    hr_index = jnp.sum(is_here * jnp.where(is_used, hr_index, 2 * HALF)[None, :], axis=1)
    rows = jnp.arange(2 * HALF, dtype=jnp.int32)
    upto = jnp.sum((key[None, :] <= rows[:, None]).astype(jnp.int32), axis=1)
    has = jnp.any(key[None, :] == rows[:, None], axis=1)
    last = jnp.where(has, upto - 1, SLOTS)

    smem = pl.BlockSpec(memory_space=pltpu.SMEM)
    vmem = pl.BlockSpec(memory_space=pltpu.VMEM)
    f32 = jnp.float32
    dma = pltpu.SemaphoreType.DMA
    flux, cond = pl.pallas_call(
        kernel,
        out_shape=(
            jax.ShapeDtypeStruct((TEMPS, COLORS * TILE), f32),
            jax.ShapeDtypeStruct((1, TILE), f32),
        ),
        in_specs=[smem] * 5 + [pl.BlockSpec(memory_space=pl.ANY)] + [vmem] * 3,
        out_specs=(vmem, vmem),
        scratch_shapes=[
            pltpu.VMEM((SLOTS, TILE, TILE), f32),
            pltpu.VMEM((SLOTS, 2 * TILE, TILE), jnp.bfloat16),
            pltpu.VMEM((2 * HALF, TEMPS, TILE), f32),
            pltpu.VMEM((SLOTS + 1, TEMPS, TILE), f32),
            pltpu.VMEM((HALF, TEMPS, TILE), f32),
            pltpu.VMEM((HALF, TEMPS, TILE), f32),
            pltpu.VMEM((HALF, TEMPS, TILE), f32),
            pltpu.VMEM((COLORS * RING_TILES, TEMPS, TILE), f32),
            pltpu.VMEM((2 * HALF + 1, 1, TILE), f32),
            pltpu.VMEM((TEMPS, TILE), f32),
            pltpu.VMEM((16, 8, TILE), f32),
            dma,
            dma((COLORS, 3)),
            dma((COLORS, 3)),
            dma((COLORS, 2, 5)),
            dma((COLORS, 2, 5)),
            dma((COLORS, 4, 2, 2)),
            dma((COLORS, 4, 2, 2)),
            dma((COLORS, 13)),
            dma((COLORS, 13)),
            dma((COLORS, 4, 4)),
            dma((COLORS, 4, 4)),
            dma((COLORS, 4, 2, 2)),
            dma((COLORS, 4, 2, 2)),
            dma((COLORS, 2, 5)),
            dma((COLORS, 2, 5)),
            dma((COLORS, 3)),
            dma((COLORS, 3)),
            dma((4, 3)),
            dma((4, 3)),
            dma((3, 7)),
            dma((3, 7)),
        ],
        compiler_params=pltpu.CompilerParams(
            collective_id=0, has_side_effects=True, vmem_limit_bytes=67043328
        ),
        name="solve",
    )(
        order,
        xs,
        keys,
        hr_index,
        last,
        tile_values,
        driving.T,
        relaxation,
        heat_weight,
    )
    return flux.T, cond[0, :TEMPS]


def solution(mesh):
    torus = Mesh(mesh.devices.reshape(4, 4, 4, 2), AXES)
    placed = (
        P(AXES, None, None),
        P(AXES, None),
        P(AXES),
        P(AXES),
        P(AXES),
        P(AXES),
        P(AXES, None),
        P(AXES),
    )
    return jax.shard_map(
        shards, mesh=torus, in_specs=placed, out_specs=(P(AXES, None), P()), check_vma=False
    )
```

```python
import jax
import jax.numpy as jnp
from jax import lax
from jax.experimental import pallas as pl
from jax.experimental.pallas import tpu as pltpu
from jax.sharding import Mesh
from jax.sharding import PartitionSpec as P

ITERS = 3
TILE = 128
TEMPS = 64
ROWT_DEV = 24
SLOTS = 128
RING = 4
CHIPS = 64
COLORS = 3
HALF = COLORS * CHIPS
AXES = ("z", "y", "x", "core")
ORDERS = (("x", "y", "z"), ("y", "z", "x"), ("z", "x", "y"))
GROUPS = (2, 1, 3, 0)
RING_TILES = 63
NT = (((1,), (1,)), ((), ()))
NN = (((1,), (0,)), ((), ()))
STEPS = (1, 3, 2)
PARTS = 4
MESH = pl.DeviceIdType.MESH


def place(coords, color, strides):
    order = ORDERS[color]
    return coords[order[0]] + strides[0] * coords[order[1]] + strides[1] * coords[order[2]]


X_STRIDES = (4, 16)
Y_STRIDES = (16, 4)


def kernel(
    order_ref,
    xs_ref,
    keys_ref,
    hr_index_ref,
    last_ref,
    tiles_hbm,
    driving_ref,
    relax_ref,
    heat_ref,
    flux_ref,
    cond_ref,
    stage,
    t_both,
    x_all,
    sums,
    y_own,
    y_pair,
    r_pair,
    r_ring,
    hr_all,
    part_ref,
    c_all,
    stage_sem,
    g1_send,
    g1_recv,
    g2_send,
    g2_recv,
    g3_send,
    g3_recv,
    fw_send,
    fw_recv,
    pr_send,
    pr_recv,
    s3_send,
    s3_recv,
    s2_send,
    s2_recv,
    s1_send,
    s1_recv,
    h_send,
    h_recv,
    c_send,
    c_recv,
):
    coords = {a: lax.axis_index(a) for a in AXES}
    core = coords["core"]
    mate = {"core": 1 - core}

    def at(axis, step):
        return {axis: lax.rem(coords[axis] + step, RING)}

    def chip_row(k):
        spot = lax.rem(coords["x"] * 2 + core + k, 8)
        return {"x": spot // 2, "core": lax.rem(spot, 2)}

    peers = [at(axis, step) for axis in ("y", "z") for step in (1, 2, 3)]
    peers += [chip_row(k) for k in range(1, 8)]
    barrier = pltpu.get_barrier_semaphore()
    for peer in peers:
        pl.semaphore_signal(barrier, inc=1, device_id=peer, device_id_type=MESH)
    load = pltpu.make_async_copy(tiles_hbm, stage, stage_sem)
    load.start()

    def lanes(c):
        return slice(c * TILE, (c + 1) * TILE)

    def relax(c):
        return relax_ref[lanes(c)].reshape(1, TILE)

    def heat(c):
        return heat_ref[lanes(c)].reshape(1, TILE)

    h_base = core * HALF
    h_own = h_base + place(coords, 0, X_STRIDES) * COLORS

    own = [(c * 2 + core) * CHIPS + place(coords, c, X_STRIDES) for c in range(COLORS)]
    for c in range(COLORS):
        x_all[own[c]] = relax(c) * driving_ref[:, lanes(c)]
        hr_all[h_own + c] = heat(c) * relax(c)
    sums[SLOTS] = jnp.zeros((TEMPS, TILE), jnp.float32)
    hr_all[2 * HALF] = jnp.zeros((1, TILE), jnp.float32)
    pl.semaphore_wait(barrier, len(peers))

    def along(c, p, step):
        return lax.rem(coords[ORDERS[c][p]] + step, RING)

    sends = []

    def plain(src, dst, ssem, rsem, device):
        return pltpu.make_async_remote_copy(
            src_ref=src, dst_ref=dst, send_sem=ssem, recv_sem=rsem, device_id=device, device_id_type=MESH
        )

    def remote(*args):
        copy = plain(*args)
        copy.start()
        sends.append(copy)
        return copy

    def drain(count):
        for copy in sends[:count]:
            copy.wait_send()
        del sends[:count]

    def to(c, p, way):
        return at(ORDERS[c][p], 1 + 2 * way)

    def split_tiles(part):
        if part == 0:
            load.wait()

        @pl.loop(part * SLOTS // PARTS, (part + 1) * SLOTS // PARTS)
        def _(j):
            tile = stage[order_ref[j]].T
            hi = tile.astype(jnp.bfloat16)
            t_both[j, :TILE] = hi
            t_both[j, TILE:] = (tile - hi.astype(jnp.float32)).astype(jnp.bfloat16)

    def weights(stage_of):
        axis = ("x", "y", "z")[stage_of]
        first = h_base + COLORS * (
            coords["x"] * (stage_of < 1) + coords["y"] * 4 * (stage_of < 2) + coords["z"] * 16
        )
        ref = hr_all.at[pl.ds(first, COLORS * 4**stage_of)]
        return [
            plain(ref, ref, h_send.at[stage_of, step - 1], h_recv.at[stage_of, step - 1], at(axis, step))
            for step in STEPS
        ]

    def weights_to_mate():
        ref = hr_all.at[pl.ds(h_base, HALF)]
        return [plain(ref, ref, h_send.at[3, 0], h_recv.at[3, 0], mate)]

    def start(copies):
        for copy in copies:
            copy.start()

    def receive(copies):
        for copy in copies:
            copy.wait_recv()

    def first_only(sweep, *acts):
        @pl.when(sweep == 0)
        def _():
            for act in acts:
                act()

    everyone = range(COLORS)
    ways = (0, 1)

    def gather(sweep):
        near, far, wide, forwards = {}, {}, {}, []
        wide2 = {}

        def xt(c, j, g):
            return (c * 2 + core) * CHIPS + along(c, 2, j) * 16 + along(c, 1, g) * 4

        def tiles(first, count):
            return x_all.at[pl.ds(first, count)]

        def forward(c, piece, first, count):
            ref = tiles(first, count)
            forwards.append(remote(ref, ref, fw_send.at[c, piece], fw_recv.at[c, piece], mate))

        def block(c, g):
            for w in ways:
                ref = tiles(xt(c, 0, g), 4)
                wide[c, g, w] = remote(ref, ref, g3_send.at[c, g, w, 0], g3_recv.at[c, g, w, 0], to(c, 2, w))

        def relay(c, g):
            for w in ways:
                wide[c, g, w].wait_recv()
                ref = tiles(xt(c, 3 - 2 * w, g) + 2 * w, 2)
                wide2[c, g, w] = remote(ref, ref, g3_send.at[c, g, w, 1], g3_recv.at[c, g, w, 1], to(c, 2, w))
            for w in ways:
                forward(c, 1 + g * 3 + w, xt(c, 3 - 2 * w, g), 4)

        def arrived(c, g):
            for w in ways:
                wide2[c, g, w].wait_recv()
            forward(c, 3 + g * 3, xt(c, 2, g), 4)

        for c in everyone:
            for step in (1, 3, 2):
                ref = tiles(own[c], 1)
                near[c, step] = remote(
                    ref, ref, g1_send.at[c, step - 1], g1_recv.at[c, step - 1], at(ORDERS[c][0], step)
                )
        def send2(c, i, k):
            ref = tiles(xt(c, 0, 0) + along(c, 0, k), 1)
            for w in ways:
                far[c, w, i] = remote(ref, ref, g2_send.at[c, w, 1 + i], g2_recv.at[c, w, 1 + i], to(c, 1, w))

        for c in everyone:
            send2(c, 0, 0)
        for step in (1, 3, 2):
            for c in everyone:
                near[c, step].wait_recv()
                send2(c, step, 4 - step)
        for c in everyone:
            block(c, 0)
        first_only(sweep, lambda: receive(weights(0)), lambda: start(weights(1)), lambda: split_tiles(0))
        for c in everyone:
            for w in ways:
                for i in range(4):
                    far[c, w, i].wait_recv()
                ref = tiles(xt(c, 0, 3 - 2 * w) + 2 * w, 2)
                far[c, w] = remote(ref, ref, g2_send.at[c, w, 0], g2_recv.at[c, w, 0], to(c, 1, w))
        for g in (3, 1):
            for c in everyone:
                block(c, g)
        first_only(sweep, lambda: receive(weights(1)), lambda: start(weights(2)), lambda: split_tiles(1))
        for c in everyone:
            relay(c, 0)
        for c in everyone:
            for w in ways:
                far[c, w].wait_recv()
            block(c, 2)
            forward(c, 0, (c * 2 + core) * CHIPS + along(c, 2, 0) * 16, 16)
        first_only(sweep, lambda: receive(weights(2)), lambda: start(weights_to_mate()), lambda: split_tiles(2))
        for g in (3, 1):
            for c in everyone:
                relay(c, g)
        for c in everyone:
            arrived(c, 0)
        for c in everyone:
            relay(c, 2)
        first_only(sweep, lambda: split_tiles(3))
        for g in (3, 1, 2):
            for c in everyone:
                arrived(c, g)
        first_only(sweep, lambda: receive(weights_to_mate()))
        for copy in forwards:
            copy.wait_recv()

    def multiply():
        unroll = 32

        def some(g, carry):
            acc, part = carry
            for u in range(unroll):
                j = g * unroll + u
                x = x_all[xs_ref[j]]
                hi = x.astype(jnp.bfloat16)
                lo = (x - hi.astype(jnp.float32)).astype(jnp.bfloat16)
                prod = lax.dot_general(
                    jnp.concatenate([hi, hi], axis=1), t_both[j], NN, preferred_element_type=jnp.float32
                ) + lax.dot_general(lo, t_both[j, :TILE], NN, preferred_element_type=jnp.float32)
                acc = jnp.where(keys_ref[j] != keys_ref[lax.max(j - 1, 0)], 0.0, acc) + prod
                part = part + prod * hr_all[hr_index_ref[j]]
                sums[j] = acc
            return acc, part

        zero = jnp.zeros((TEMPS, TILE), jnp.float32)
        part_ref[...] = lax.fori_loop(0, SLOTS // unroll, some, (zero, zero))[1]

    row = [chip_row(k) for k in range(8)]
    rounds = (
        (0, 8, coords["x"] * 2 + core, row[1:]),
        (8, RING, coords["y"], [at("y", k) for k in (1, 2, 3)]),
        (12, RING, coords["z"], [at("z", k) for k in (1, 2, 3)]),
    )

    def totals(k):
        base, _, here, others = rounds[k]
        ref = c_all.at[base + here]
        return [plain(ref, ref, c_send.at[k, i], c_recv.at[k, i], peer) for i, peer in enumerate(others)]

    def first_total():
        part, weight = part_ref[...], 0.0
        for c in range(COLORS):
            part = part + heat(c) * relax(c) * driving_ref[:, lanes(c)]
            weight = weight + heat(c)
        ones = jnp.ones((8, TILE), jnp.float32)

        def lane_sum(rows):
            return lax.dot_general(
                ones, rows, NT, precision=lax.Precision.HIGHEST, preferred_element_type=jnp.float32
            )

        over = lane_sum(jnp.concatenate([part, part], axis=0))
        under = lane_sum(jnp.broadcast_to(weight, (TILE, TILE)))
        upper = lax.broadcasted_iota(jnp.int32, (8, TILE), 0) < 4
        return jnp.where(upper, over, under)

    def round_total(k):
        base, size = rounds[k][:2]
        receive(totals(k))
        total = c_all[base]
        for i in range(1, size):
            total = total + c_all[base + i]
        return total

    def start_round(k):
        c_all[rounds[k][0] + rounds[k][2]] = first_total() if k == 0 else round_total(k - 1)
        start(totals(k))

    def last_only(sweep, act):
        pl.when(sweep == ITERS - 1)(act)

    def scatter(sweep):
        gather_sends = len(sends)
        pair, half, full, tail, last = {}, {}, {}, {}, {}

        def yt(c, g, j):
            return c * CHIPS + along(c, 1, g) * 16 + along(c, 2, j) * 4

        def rt(c, g):
            return c * RING_TILES + g * 12

        def give(c, g, j):
            first = yt(c, g, j)
            for u in range(4):
                y_pair[first + u] = sums[last_ref[c * CHIPS + (1 - core) * CHIPS + first + u]]
            span = pl.ds(first, 4)
            pair[c, g, j] = remote(y_pair.at[span], r_pair.at[span], pr_send.at[c, g, j], pr_recv.at[c, g, j], mate)

        def both_cores(c, g, j):
            first = yt(c, g, j)
            pair[c, g, j].wait_recv()
            return first, [
                sums[last_ref[c * CHIPS + core * CHIPS + first + u]] + r_pair[first + u] for u in range(4)
            ]

        def take(c, g):
            first, rows = both_cores(c, g, 2)
            for u in range(4):
                y_own[first + u] = rows[u]
            for w in ways:
                half[c, g, w] = remote(
                    y_own.at[pl.ds(first + 2 * w, 2)],
                    r_ring.at[pl.ds(rt(c, g) + 2 * w, 2)],
                    s3_send.at[c, g, w, 0],
                    s3_recv.at[c, g, w, 0],
                    to(c, 2, w),
                )

        def pass_on(c, g):
            for w in ways:
                near, rows = both_cores(c, g, 1 + 2 * w)
                half[c, g, w].wait_recv()
                for u in range(4):
                    y_own[near + u] = rows[u] + r_ring[rt(c, g) + u] if u // 2 == w else rows[u]
                full[c, g, w] = remote(
                    y_own.at[pl.ds(near, 4)],
                    r_ring.at[pl.ds(rt(c, g) + 4 + 4 * w, 4)],
                    s3_send.at[c, g, w, 1],
                    s3_recv.at[c, g, w, 1],
                    to(c, 2, w),
                )

        def settle(c, g):
            here, rows = both_cores(c, g, 0)
            for w in ways:
                full[c, g, w].wait_recv()
            for u in range(4):
                y_own[here + u] = rows[u] + (r_ring[rt(c, g) + 4 + u] + r_ring[rt(c, g) + 8 + u])

        def take2(c):
            for w in ways:
                half[c, w] = remote(
                    y_own.at[pl.ds(yt(c, 2, 0) + 2 * w, 2)],
                    r_ring.at[pl.ds(rt(c, 4) + 2 * w, 2)],
                    s2_send.at[c, w, 0],
                    s2_recv.at[c, w, 0],
                    to(c, 1, w),
                )

        def pass_on2(c):
            for w in ways:
                half[c, w].wait_recv()
                near = yt(c, 1 + 2 * w, 0)
                for u in range(2 * w, 2 * w + 2):
                    y_own[near + u] = y_own[near + u] + r_ring[rt(c, 4) + u]
            for step in (2, 1, 3, 0):
                for w in ways:
                    k = along(c, 0, step)
                    tail[c, w, step] = remote(
                        y_own.at[pl.ds(yt(c, 1 + 2 * w, 0) + k, 1)],
                        r_ring.at[pl.ds(rt(c, 4) + 4 + 4 * w + k, 1)],
                        s2_send.at[c, w, 1 + step],
                        s2_recv.at[c, w, 1 + step],
                        to(c, 1, w),
                    )

        def settle2(c, step):
            for w in ways:
                tail[c, w, step].wait_recv()
            k = along(c, 0, step)
            here = yt(c, 0, 0) + k
            y_own[here] = y_own[here] + (r_ring[rt(c, 4) + 4 + k] + r_ring[rt(c, 4) + 8 + k])
            if step:
                last[c, step] = remote(
                    y_own.at[pl.ds(here, 1)],
                    r_ring.at[pl.ds(rt(c, 5) + step - 1, 1)],
                    s1_send.at[c, step - 1],
                    s1_recv.at[c, step - 1],
                    at(ORDERS[c][0], step),
                )

        for j, groups in ((2, GROUPS), (1, (2,)), (3, (2,)), (1, (1,)), (3, (1,)), (1, (3,)), (3, (3,))):
            for g in groups:
                for c in everyone:
                    give(c, g, j)
        for j, groups in ((0, (2,)), (1, (0,)), (3, (0,)), (0, (1, 3, 0))):
            for g in groups:
                for c in everyone:
                    give(c, g, j)
        plan = (
            (take, 2),
            (take, 1),
            (take, 3),
            (take, 0),
            (pass_on, 2),
            (pass_on, 1),
            (pass_on, 3),
            (settle, 2),
            (take2,),
            (pass_on, 0),
            (settle, 1),
            (settle, 3),
            (pass_on2,),
            (settle, 0),
            (settle2, 2),
            (settle2, 1),
            (settle2, 3),
            (settle2, 0),
        )
        for k, (act, *group) in enumerate(plan):
            for c in everyone:
                act(c, *group)
            if k == 6:
                drain(gather_sends)
            if k in (3, 7, 10):
                last_only(sweep, lambda k=k: start_round((3, 7, 10).index(k)))
        drain(len(sends) - 3 * COLORS)
        for c in everyone:
            for step in (1, 3, 2):
                last[c, step].wait_recv()
            got = (r_ring[rt(c, 5)] + r_ring[rt(c, 5) + 1]) + r_ring[rt(c, 5) + 2]
            total = y_own[yt(c, 0, 0) + along(c, 0, 0)] + got
            flux = relax(c) * (driving_ref[:, lanes(c)] + total)
            flux_ref[:, lanes(c)] = flux
            x_all[own[c]] = flux
        drain(len(sends))

    def sweep_once(sweep, carry):
        gather(sweep)
        multiply()
        scatter(sweep)
        return carry

    start(weights(0))
    lax.fori_loop(0, ITERS, sweep_once, 0)

    total = round_total(2)
    cond_ref[...] = total[0:1] / total[4:5]
    for k in range(3):
        for copy in totals(k) + weights(k):
            copy.wait_send()
    weights_to_mate()[0].wait_send()


def index_of(device, color, strides):
    coords = {"z": device // 32, "y": device // 8 % 4, "x": device // 2 % 4}
    spots = [place(coords, c, strides) for c in range(COLORS)]
    spot = jnp.where(color == 0, spots[0], jnp.where(color == 1, spots[1], spots[2]))
    return (color * 2 + device % 2) * CHIPS + spot


def shards(tile_values, tile_owner, tile_row, tile_col, tile_count, relaxation, driving, heat_weight):
    owner = tile_owner[:, 0]
    slots = jnp.arange(SLOTS, dtype=jnp.int32)
    is_used = slots < tile_count[0]
    row = (owner // 8) * ROWT_DEV + tile_row
    key = jnp.where(is_used, index_of(row // COLORS, row % COLORS, Y_STRIDES), 2 * HALF)
    xs = index_of((tile_col // COLORS) * 8 + owner % 8, tile_col % COLORS, X_STRIDES)
    before = (key[None, :] < key[:, None]) | ((key[None, :] == key[:, None]) & (slots[None, :] < slots[:, None]))
    rank = jnp.sum(before.astype(jnp.int32), axis=1)
    is_here = (rank[None, :] == slots[:, None]).astype(jnp.int32)
    order = jnp.sum(is_here * slots[None, :], axis=1)
    xs = jnp.sum(is_here * xs[None, :], axis=1)
    keys = jnp.sum(is_here * key[None, :], axis=1)
    device, color = row // COLORS, row % COLORS
    spot = {"z": device // 32, "y": device // 8 % 4, "x": device // 2 % 4}
    hr_index = (device % 2 * CHIPS + place(spot, 0, X_STRIDES)) * COLORS + color
    hr_index = jnp.sum(is_here * jnp.where(is_used, hr_index, 2 * HALF)[None, :], axis=1)
    rows = jnp.arange(2 * HALF, dtype=jnp.int32)
    upto = jnp.sum((key[None, :] <= rows[:, None]).astype(jnp.int32), axis=1)
    has = jnp.any(key[None, :] == rows[:, None], axis=1)
    last = jnp.where(has, upto - 1, SLOTS)

    smem = pl.BlockSpec(memory_space=pltpu.SMEM)
    vmem = pl.BlockSpec(memory_space=pltpu.VMEM)
    f32 = jnp.float32
    dma = pltpu.SemaphoreType.DMA
    flux, cond = pl.pallas_call(
        kernel,
        out_shape=(
            jax.ShapeDtypeStruct((TEMPS, COLORS * TILE), f32),
            jax.ShapeDtypeStruct((1, TILE), f32),
        ),
        in_specs=[smem] * 5 + [pl.BlockSpec(memory_space=pl.ANY)] + [vmem] * 3,
        out_specs=(vmem, vmem),
        scratch_shapes=[
            pltpu.VMEM((SLOTS, TILE, TILE), f32),
            pltpu.VMEM((SLOTS, 2 * TILE, TILE), jnp.bfloat16),
            pltpu.VMEM((2 * HALF, TEMPS, TILE), f32),
            pltpu.VMEM((SLOTS + 1, TEMPS, TILE), f32),
            pltpu.VMEM((HALF, TEMPS, TILE), f32),
            pltpu.VMEM((HALF, TEMPS, TILE), f32),
            pltpu.VMEM((HALF, TEMPS, TILE), f32),
            pltpu.VMEM((COLORS * RING_TILES, TEMPS, TILE), f32),
            pltpu.VMEM((2 * HALF + 1, 1, TILE), f32),
            pltpu.VMEM((TEMPS, TILE), f32),
            pltpu.VMEM((16, 8, TILE), f32),
            dma,
            dma((COLORS, 3)),
            dma((COLORS, 3)),
            dma((COLORS, 2, 5)),
            dma((COLORS, 2, 5)),
            dma((COLORS, 4, 2, 2)),
            dma((COLORS, 4, 2, 2)),
            dma((COLORS, 13)),
            dma((COLORS, 13)),
            dma((COLORS, 4, 4)),
            dma((COLORS, 4, 4)),
            dma((COLORS, 4, 2, 2)),
            dma((COLORS, 4, 2, 2)),
            dma((COLORS, 2, 5)),
            dma((COLORS, 2, 5)),
            dma((COLORS, 3)),
            dma((COLORS, 3)),
            dma((4, 3)),
            dma((4, 3)),
            dma((3, 7)),
            dma((3, 7)),
        ],
        compiler_params=pltpu.CompilerParams(
            collective_id=0, has_side_effects=True, vmem_limit_bytes=67043328
        ),
        name="solve",
    )(
        order,
        xs,
        keys,
        hr_index,
        last,
        tile_values,
        driving.T,
        relaxation,
        heat_weight,
    )
    return flux.T, cond[0, :TEMPS]


def solution(mesh):
    torus = Mesh(mesh.devices.reshape(4, 4, 4, 2), AXES)
    placed = (
        P(AXES, None, None),
        P(AXES, None),
        P(AXES),
        P(AXES),
        P(AXES),
        P(AXES),
        P(AXES, None),
        P(AXES),
    )
    return jax.shard_map(
        shards, mesh=torus, in_specs=placed, out_specs=(P(AXES, None), P()), check_vma=False
    )
```
